512 devices in a mesh: row: 16 (over z), col: 8 (over x, y_hi), depth: 4 (over y_lo, core).
Axes of the slice: x: 4, y: 4 (y_hi: 2, y_lo: 2; y = y_hi * 2 + y_lo), z: 16, core: 2. Of those that a mesh axis runs over, the one named last changes fastest.
Arguments:
- a_vals: bfloat16 [16, 4, 8, 4, 128, 128], P('row', 'depth', 'col'), may hold values from 0.02 to 14.4, as said below
- a_rows: int32 [16, 4, 8, 4], P('row', 'depth', 'col'), may hold values from 0 to 1, as said below
- a_cols: int32 [16, 4, 8, 4], P('row', 'depth', 'col'), may hold values from 0 to 31, as said below
- a_count: int32 [16, 4, 8], P('row', 'depth', 'col'), may hold values from 1 to 4, as said below
- b_vals: bfloat16 [4, 16, 8, 12, 128, 128], P('depth', 'row', 'col'), may hold values from 0.019897461 to 0.5
- b_rows: int32 [4, 16, 8, 12], P('depth', 'row', 'col'), may hold values from 0 to 15, as said below
- b_cols: int32 [4, 16, 8, 12], P('depth', 'row', 'col'), may hold values from 0 to 7, as said below
- b_count: int32 [4, 16, 8], P('depth', 'row', 'col'), may hold values from 1 to 12, as said below
- keep: int32 [32, 8192], P('row', ('col', 'depth')), may hold values 0 or 1
Outputs:
- flow: float32 [4096, 8192], P('row', ('col', 'depth'))
The draws below stay inside these ranges and needn't reach their ends.
Inputs may be any that keep to these rules, and one draw needn't show every extreme that they name: a_rows and a_cols name the block position of each slot of a left tile; the 4 slots of a tile, padding included, hold distinct positions. `a_cols`: see a_rows. `a_count`: live slots of a left tile; some tile is full. b_rows and b_cols name the block position of each slot of a right tile; the 12 slots of a tile, padding included, hold distinct positions. `b_cols`: see b_rows. `b_count`: live slots of a right tile; some tile is full. `a_vals`: positive block entries.
All inputs are finite; a program needn't handle non-finite values. No bound on the sum of `keep` on one device may be relied on, other than what follows from the above.
Results may differ from the reference program's by a relative error of at most 0.0003.
Values may be sent and summed in bfloat16 or wider, within the bound.
A program may use at most 128 MiB of HBM per device.

```python
import math
import jax
import jax.numpy as jnp
from jax import lax

BS = 128
ROWB = 2
KT = 32
COLB = 8
KBT = 16
NZA = 4
NZB = 12
N_ROW = 16
N_COL = 8
N_DEPTH = 4


def tile_places(key, salt, tiles_shape, slots, taken):
    folded = jax.random.fold_in(key, salt)
    tiles = math.prod(tiles_shape)
    subkeys = jax.random.split(folded, tiles)
    places = jax.vmap(lambda one_key: jax.random.permutation(one_key, slots)[:taken])(subkeys)
    return places.reshape(tiles_shape + (taken,)).astype(jnp.int32)


def tile_counts(key, salt, tiles_shape, most):
    folded = jax.random.fold_in(key, salt)
    first_key, second_key, third_key = jax.random.split(folded, 3)
    counts = jnp.minimum(jax.random.randint(first_key, tiles_shape, 1, most + 1), jax.random.randint(second_key, tiles_shape, 1, most + 1))
    flat_counts = counts.reshape(-1)
    chosen = jax.random.randint(third_key, (), 0, flat_counts.shape[0])
    flat_counts = flat_counts.at[chosen].set(most)
    return flat_counts.reshape(tiles_shape).astype(jnp.int32)


def draw_a_vals(key, part):
    shape = (N_ROW, N_DEPTH, N_COL, NZA, BS, BS)
    first_key, second_key = jax.random.split(jax.random.fold_in(key, 5))
    base = jnp.exp(jax.random.uniform(first_key, shape, jnp.float32, math.log(0.02), math.log(0.3)))
    scale = jnp.exp(jax.random.uniform(second_key, shape[:-1] + (1,), jnp.float32, 0.0, math.log(10.0)))
    trend = 1.0 + 2.0 * jnp.arange(N_ROW, dtype=jnp.float32).reshape(N_ROW, 1, 1, 1, 1, 1) / (N_ROW - 1)
    return (base * scale * trend).astype(jnp.bfloat16)


def draw_a_rows(key, part):
    places = tile_places(key, 11, (N_ROW, N_DEPTH, N_COL), ROWB * KT, NZA)
    return (places // KT).astype(jnp.int32)


def draw_a_cols(key, part):
    places = tile_places(key, 11, (N_ROW, N_DEPTH, N_COL), ROWB * KT, NZA)
    return (places % KT).astype(jnp.int32)


def draw_a_count(key, part):
    return tile_counts(key, 31, (N_ROW, N_DEPTH, N_COL), NZA)


def draw_b_rows(key, part):
    places = tile_places(key, 23, (N_DEPTH, N_ROW, N_COL), KBT * COLB, NZB)
    return (places // COLB).astype(jnp.int32)


def draw_b_cols(key, part):
    places = tile_places(key, 23, (N_DEPTH, N_ROW, N_COL), KBT * COLB, NZB)
    return (places % COLB).astype(jnp.int32)


def draw_b_count(key, part):
    return tile_counts(key, 37, (N_DEPTH, N_ROW, N_COL), NZB)


def place_ends(result, key, smallest, high):
    longest = result.shape.index(max(result.shape))
    spots = []
    for shift in (0, 1):
        where = [jax.random.randint(jax.random.fold_in(key, axis), (), 0, length) for axis, length in enumerate(result.shape)]
        where[longest] = (where[longest] + shift) % result.shape[longest]
        spots.append(tuple(where))
    return result.at[spots[0]].set(smallest).at[spots[1]].set(high)


def levels(stream_key, dims, pieces, smallest, top_value):
    def one(axis_at, blocks):
        steps = jax.random.uniform(jax.random.fold_in(jax.random.fold_in(stream_key, 6), axis_at), (blocks,), jnp.float32, smallest / len(pieces), top_value / len(pieces))
        return jnp.repeat(jnp.exp(steps), dims[axis_at] // blocks).reshape((-1,) + (1,) * (len(dims) - axis_at - 1))

    gain = one(*pieces[0])
    for cut in pieces[1:]:
        gain = gain * one(*cut)
    return gain


def setup_inputs(seed: int = 0) -> dict:
    key_of = jax.random.split(jax.random.key(seed), 10)
    a_vals = draw_a_vals(jax.random.fold_in(key_of[9], 71), 0)
    a_rows = draw_a_rows(jax.random.fold_in(key_of[9], 71), 0)
    a_cols = draw_a_cols(jax.random.fold_in(key_of[9], 71), 0)
    a_count = draw_a_count(jax.random.fold_in(key_of[9], 71), 0)
    b_vals = jnp.clip(jnp.exp(math.log(0.5) - 3.224016 * jax.random.uniform(key_of[4], (N_DEPTH, N_ROW, N_COL, NZB, BS, BS), jnp.float32) ** levels(key_of[4], (N_DEPTH, N_ROW, N_COL, NZB, BS, BS), ((0, 4), (1, 16), (2, 8)), -0.2, 0.2)), 0.019897461, 0.5).astype(jnp.bfloat16)
    b_rows = draw_b_rows(jax.random.fold_in(key_of[9], 71), 0)
    b_cols = draw_b_cols(jax.random.fold_in(key_of[9], 71), 0)
    b_count = draw_b_count(jax.random.fold_in(key_of[9], 71), 0)
    keep = place_ends((jax.random.randint(key_of[8], (N_ROW * ROWB, N_COL * COLB * BS), 0, 4) < 3).astype(jnp.int32), jax.random.fold_in(key_of[8], 1), 0, 1)
    return {"a_vals": a_vals, "a_rows": a_rows, "a_cols": a_cols, "a_count": a_count, "b_vals": b_vals, "b_rows": b_rows, "b_cols": b_cols, "b_count": b_count, "keep": keep}


epsilon = 1e-6


def reference(a_vals, a_rows, a_cols, a_count, b_vals, b_rows, b_cols, b_count, keep):
    active = jnp.arange(NZA, dtype=jnp.int32)[None, None, None, :] < a_count[..., None]
    masked_a = jnp.where(active[..., None, None], a_vals, jnp.zeros_like(a_vals))
    active_b = jnp.arange(NZB, dtype=jnp.int32)[None, None, None, :] < b_count[..., None]
    masked_b = jnp.where(active_b[..., None, None], b_vals, jnp.zeros_like(b_vals))
    row_ranks = jnp.arange(ROWB, dtype=jnp.int32)

    def column_block(col_index):
        def layer(total, depth_index):
            vals_b = masked_b[depth_index, :, col_index]
            inner_b = (jnp.arange(N_ROW, dtype=jnp.int32)[:, None] * KBT + b_rows[depth_index, :, col_index]).astype(jnp.int32)
            cols_b = b_cols[depth_index, :, col_index].astype(jnp.int32)
            dense = jnp.zeros((KBT * N_ROW, COLB, BS, BS), vals_b.dtype).at[inner_b, cols_b].add(vals_b)
            dense = dense.transpose(0, 2, 1, 3).reshape(KBT * N_ROW, BS, COLB * BS)

            def row_part(row_index):
                vals_a = masked_a[row_index, depth_index].reshape(N_COL * NZA, BS, BS)
                inner_a = (jnp.arange(N_COL, dtype=jnp.int32)[:, None] * KT + a_cols[row_index, depth_index]).reshape(-1).astype(jnp.int32)
                picked = dense[inner_a]
                terms = jnp.einsum("sha,sax->shx", vals_a.astype(jnp.float32), picked.astype(jnp.float32))
                onehot = (a_rows[row_index, depth_index].reshape(-1)[:, None] == row_ranks[None, :]).astype(jnp.float32)
                return jnp.einsum("sr,shx->rhx", onehot, terms, precision=lax.Precision.HIGHEST)

            parts = lax.map(row_part, jnp.arange(N_ROW, dtype=jnp.int32))
            return total + parts, None

        start = jnp.zeros((N_ROW, ROWB, BS, COLB * BS), jnp.float32)
        total, _ = lax.scan(layer, start, jnp.arange(N_DEPTH, dtype=jnp.int32))
        return total

    blocks = lax.map(column_block, jnp.arange(N_COL, dtype=jnp.int32))
    product = blocks.transpose(1, 2, 3, 0, 4).reshape(N_ROW * ROWB, BS, N_COL * COLB * BS)
    pruned = jnp.where(keep[:, None, :] > 0, product, jnp.zeros_like(product))
    squares = pruned * pruned
    mass = jnp.mean(squares, axis=(0, 1))
    flow = squares / (mass + epsilon)
    return flow.reshape(N_ROW * ROWB * BS, N_COL * COLB * BS)
```

```python
import jax
import jax.numpy as jnp
from jax import lax
from jax.experimental import pallas as pl
from jax.experimental.pallas import tpu as pltpu
from jax.sharding import PartitionSpec as P

BS = 128
ROWB = 2
KT = 32
COLB = 8
KBT = 16
NZA = 4
NZB = 12
N_ROW = 16
N_COL = 8
N_DEPTH = 4
HALF = NZB // 2
FAR = N_ROW // 2
ABSENT = NZB
LANES = 128
QUARTER = COLB * BS // N_DEPTH
ROWS = ROWB * BS
RIGHT, LEFT = 0, 1

epsilon = 1e-06
MESH = pl.DeviceIdType.MESH


def kernel(a_hbm, akey_ref, b_hbm, bkey_ref, keep_ref, sq_ref, mass_ref, *scratch):
    tiles = scratch[:N_ROW]
    (abuf, lhs, akeys, bkeys, table, table_s, acc, rs1, rs2, colsum, masses,
     local_sem, ring_send, ring_recv, a_send, a_recv, ak_send, ak_recv, bk_send, bk_recv,
     d1_send, d1_recv, d2_send, d2_recv, m_send, m_recv) = scratch[N_ROW:]
    row = lax.axis_index("row")
    col = lax.axis_index("col")
    depth = lax.axis_index("depth")
    y_lo, core = depth // 2, depth % 2
    sibling = y_lo * 2 + (1 - core)
    across = (1 - y_lo) * 2 + core
    across_sibling = (1 - y_lo) * 2 + (1 - core)

    def row_peer(k):
        return lax.rem(row + k, N_ROW)

    def col_peer(k):
        return lax.rem(col + k, N_COL)

    own_b = pltpu.make_async_copy(b_hbm, tiles[0].at[pl.ds(0, NZB)], local_sem.at[0])
    own_b.start()
    own_a = pltpu.make_async_copy(a_hbm, abuf.at[col], local_sem.at[1])
    own_a.start()

    barrier = pltpu.get_barrier_semaphore()
    for k in range(1, N_ROW):
        pl.semaphore_signal(barrier, inc=1, device_id={"row": row_peer(k)}, device_id_type=MESH)
    for k in range(1, N_COL):
        pl.semaphore_signal(barrier, inc=1, device_id={"col": col_peer(k)}, device_id_type=MESH)
    for other in (sibling, across):
        pl.semaphore_signal(barrier, inc=1, device_id={"depth": other}, device_id_type=MESH)
    pl.semaphore_wait(barrier, N_ROW - 1 + N_COL - 1 + 2)

    def tile_of(way, step):
        return tiles[step] if way == RIGHT or step == FAR else tiles[FAR + step]

    def hop(way, step, half):
        source = b_hbm if step == 1 else tile_of(way, step - 1)
        part = pl.ds(half * HALF, HALF)
        return pltpu.make_async_remote_copy(
            src_ref=source.at[part],
            dst_ref=tile_of(way, step).at[part],
            send_sem=ring_send.at[way, step, half],
            recv_sem=ring_recv.at[way, step, half],
            device_id={"row": row_peer(1 if way == RIGHT else N_ROW - 1)},
            device_id_type=MESH,
        )

    order = ((RIGHT, 0), (LEFT, 1), (RIGHT, 1), (LEFT, 0))

    def hops(step):
        return order if step < FAR else order[:2]

    def bkey_copy(k):
        return pltpu.make_async_remote_copy(
            src_ref=bkey_ref, dst_ref=bkeys.at[row], send_sem=bk_send.at[k], recv_sem=bk_recv.at[k],
            device_id={"row": row_peer(k)}, device_id_type=MESH)

    def akey_copy(k):
        return pltpu.make_async_remote_copy(
            src_ref=akey_ref, dst_ref=akeys.at[col], send_sem=ak_send.at[k], recv_sem=ak_recv.at[k],
            device_id={"col": col_peer(k)}, device_id_type=MESH)

    def a_copy(k):
        return pltpu.make_async_remote_copy(
            src_ref=a_hbm, dst_ref=abuf.at[col], send_sem=a_send.at[k], recv_sem=a_recv.at[k],
            device_id={"col": col_peer(k)}, device_id_type=MESH)

    for way, half in order:
        hop(way, 1, half).start()
    for k in range(1, N_ROW):
        bkey_copy(k).start()
    for k in range(1, N_COL):
        akey_copy(k).start()
    for k in range(1, N_COL):
        a_copy(k).start()

    bkeys[row] = bkey_ref[...]
    akeys[col] = akey_ref[...]
    for tile in tiles:
        tile[ABSENT] = jnp.zeros((BS, BS), jnp.bfloat16)
    acc[...] = jnp.zeros_like(acc)
    own_b.wait()
    own_a.wait()

    def prepare():
        for k in range(1, N_ROW):
            bkey_copy(k).wait_recv()
        for k in range(1, N_COL):
            akey_copy(k).wait_recv()
        lane = lax.broadcasted_iota(jnp.int32, (1, LANES), 1)
        for r in range(N_ROW):
            left = akeys[r // 2]
            wanted = left - (r % 2) * (KBT * COLB)
            have = bkeys[r]
            slot = jnp.full((1, LANES), ABSENT, jnp.int32)
            for t in range(NZB):
                slot = jnp.where(wanted == have[:, t:t + 1], t, slot)
            table[r] = jnp.where(lane < NZA * COLB, slot, left)
        move = pltpu.make_async_copy(table, table_s, local_sem.at[2])
        move.start()
        for k in range(1, N_COL):
            a_copy(k).wait_recv()
        move.wait()

        def stack(c, carry):
            for s in range(NZA):
                block = abuf[c, s]
                which = table_s[2 * c, 0, NZA * COLB + s]
                for i in range(ROWB):
                    lhs[c, i * BS:(i + 1) * BS, s * BS:(s + 1) * BS] = jnp.where(
                        which == i, block, jnp.zeros_like(block))
            return carry

        lax.fori_loop(0, N_COL, stack, 0)

    def multiply(index):
        tile = tiles[index]
        owner = lax.rem(row + (N_ROW - index if index <= FAR else index - FAR), N_ROW)
        left = lhs[owner // 2]

        def part(j, carry):
            strips = []
            for s in range(NZA):
                pair = [tile[table_s[owner, 0, s * COLB + 2 * j + e]] for e in range(2)]
                strips.append(jnp.concatenate(pair, axis=1))
            acc[j] += jnp.dot(left, jnp.concatenate(strips, axis=0), preferred_element_type=jnp.float32)
            return carry

        lax.fori_loop(0, N_DEPTH, part, 0)

    plan = {3: (0, 1, 9), 4: (2, 10, 3), 5: (11, 4, 12), 6: (5, 13), 7: (6, 14), 8: (7, 15)}
    for step in range(2, FAR + 1):
        ahead = hops(step)
        for way, half in order:
            hop(way, step - 1, half).wait_recv()
            if (way, half) in ahead:
                hop(way, step, half).start()
        if step == 3:
            prepare()
        for index in plan.get(step, ()):
            multiply(index)
    for way, half in hops(FAR):
        hop(way, FAR, half).wait_recv()
    multiply(FAR)

    def to_sibling(slot, half):
        part = pl.ds(half * BS, BS)
        which = across_sibling if slot == 0 else sibling
        return pltpu.make_async_remote_copy(
            src_ref=acc.at[which, part], dst_ref=rs1.at[slot, part],
            send_sem=d1_send.at[slot, half], recv_sem=d1_recv.at[slot, half],
            device_id={"depth": sibling}, device_id_type=MESH)

    def to_across(half):
        part = pl.ds(half * BS, BS)
        return pltpu.make_async_remote_copy(
            src_ref=acc.at[across, part], dst_ref=rs2.at[part],
            send_sem=d2_send.at[half], recv_sem=d2_recv.at[half],
            device_id={"depth": across}, device_id_type=MESH)

    for slot in range(2):
        for half in range(ROWB):
            to_sibling(slot, half).start()
    for half in range(ROWB):
        part = pl.ds(half * BS, BS)
        to_sibling(0, half).wait_recv()
        acc[across, part] += rs1[0, part]
        to_across(half).start()
    total = jnp.zeros((1, QUARTER), jnp.float32)
    for half in range(ROWB):
        part = pl.ds(half * BS, BS)
        to_sibling(1, half).wait_recv()
        mine = acc[depth, part] + rs1[1, part]
        to_across(half).wait_recv()
        product = mine + rs2[part]
        pruned = jnp.where(keep_ref[half:half + 1, :] > 0, product, 0.0)
        squares = pruned * pruned
        sq_ref[part] = squares
        total = total + jnp.sum(squares, axis=0, keepdims=True)
    colsum[...] = total
    masses[row] = total

    def mass_copy(k):
        return pltpu.make_async_remote_copy(
            src_ref=colsum, dst_ref=masses.at[row], send_sem=m_send.at[k], recv_sem=m_recv.at[k],
            device_id={"row": row_peer(k)}, device_id_type=MESH)

    for k in range(1, N_ROW):
        mass_copy(k).start()
    for k in range(1, N_ROW):
        mass_copy(k).wait_recv()
    mass_ref[...] = jnp.sum(masses[...], axis=0)

    for step in range(1, FAR + 1):
        for way, half in hops(step):
            hop(way, step, half).wait_send()
    for k in range(1, N_ROW):
        bkey_copy(k).wait_send()
        mass_copy(k).wait_send()
    for k in range(1, N_COL):
        akey_copy(k).wait_send()
        a_copy(k).wait_send()
    for half in range(ROWB):
        for slot in range(2):
            to_sibling(slot, half).wait_send()
        to_across(half).wait_send()


def shards(a_vals, a_rows, a_cols, a_count, b_vals, b_rows, b_cols, b_count, keep):
    rank = jnp.arange(COLB, dtype=jnp.int32)
    a_live = jnp.arange(NZA, dtype=jnp.int32) < a_count.reshape(())
    a_want = jnp.where(a_live[:, None], a_cols.reshape(NZA, 1) * COLB + rank[None, :], -5000)
    akey = jnp.concatenate([a_want.reshape(-1), a_rows.reshape(-1)])
    akey = jnp.pad(akey, (0, LANES - akey.shape[0]), constant_values=-5000).reshape(1, LANES)
    b_live = jnp.arange(NZB, dtype=jnp.int32) < b_count.reshape(())
    bkey = jnp.where(b_live, b_rows.reshape(NZB) * COLB + b_cols.reshape(NZB), -1000)
    bkey = jnp.pad(bkey, (0, LANES - NZB), constant_values=-1000).reshape(1, LANES)

    vmem = pl.BlockSpec(memory_space=pltpu.VMEM)
    hbm = pl.BlockSpec(memory_space=pl.ANY)
    dma = pltpu.SemaphoreType.DMA
    squares, mass = pl.pallas_call(
        kernel,
        out_shape=(
            jax.ShapeDtypeStruct((ROWS, QUARTER), jnp.float32),
            jax.ShapeDtypeStruct((1, QUARTER), jnp.float32),
        ),
        in_specs=[hbm, vmem, hbm, vmem, vmem],
        out_specs=(vmem, vmem),
        scratch_shapes=[pltpu.VMEM((NZB + 1, BS, BS), jnp.bfloat16)] * N_ROW
        + [
            pltpu.VMEM((N_COL, NZA, BS, BS), jnp.bfloat16),
            pltpu.VMEM((N_COL, ROWS, NZA * BS), jnp.bfloat16),
            pltpu.VMEM((N_COL, 1, LANES), jnp.int32),
            pltpu.VMEM((N_ROW, 1, LANES), jnp.int32),
            pltpu.VMEM((N_ROW, 1, LANES), jnp.int32),
            pltpu.SMEM((N_ROW, 1, LANES), jnp.int32),
            pltpu.VMEM((N_DEPTH, ROWS, QUARTER), jnp.float32),
            pltpu.VMEM((2, ROWS, QUARTER), jnp.float32),
            pltpu.VMEM((ROWS, QUARTER), jnp.float32),
            pltpu.VMEM((1, QUARTER), jnp.float32),
            pltpu.VMEM((N_ROW, 1, QUARTER), jnp.float32),
            dma((3,)),
            dma((2, FAR + 1, 2)),
            dma((2, FAR + 1, 2)),
            dma((N_COL,)),
            dma((N_COL,)),
            dma((N_COL,)),
            dma((N_COL,)),
            dma((N_ROW,)),
            dma((N_ROW,)),
            dma((2, ROWB)),
            dma((2, ROWB)),
            dma((ROWB,)),
            dma((ROWB,)),
            dma((N_ROW,)),
            dma((N_ROW,)),
        ],
        compiler_params=pltpu.CompilerParams(
            collective_id=0, has_side_effects=True, vmem_limit_bytes=40 << 20
        ),
    )(
        a_vals.reshape(NZA, BS, BS),
        akey,
        b_vals.reshape(NZB, BS, BS),
        bkey,
        keep,
    )
    return squares / (mass * (1.0 / (N_ROW * ROWS)) + epsilon)


def solution(mesh):
    placed = (
        P("row", "depth", "col", None, None, None),
        P("row", "depth", "col", None),
        P("row", "depth", "col", None),
        P("row", "depth", "col"),
        P("depth", "row", "col", None, None, None),
        P("depth", "row", "col", None),
        P("depth", "row", "col", None),
        P("depth", "row", "col"),
        P("row", ("col", "depth")),
    )
    return jax.shard_map(
        shards, mesh=mesh, in_specs=placed, out_specs=P("row", ("col", "depth")), check_vma=False
    )
```

```python
import jax
import jax.numpy as jnp
from jax import lax
from jax.experimental import pallas as pl
from jax.experimental.pallas import tpu as pltpu
from jax.sharding import PartitionSpec as P

BS = 128
ROWB = 2
KT = 32
COLB = 8
KBT = 16
NZA = 4
NZB = 12
N_ROW = 16
N_COL = 8
N_DEPTH = 4
HALF = NZB // 2
FAR = N_ROW // 2
ABSENT = NZB
LANES = 128
QUARTER = COLB * BS // N_DEPTH
ROWS = ROWB * BS
RIGHT, LEFT = 0, 1

epsilon = 1e-06
MESH = pl.DeviceIdType.MESH


def kernel(a_hbm, arow_hbm, acol_hbm, acount_hbm, b_hbm, brow_hbm, bcol_hbm, bcount_hbm, keep_hbm,
           flow_ref, *scratch):
    tiles = scratch[:N_ROW]
    (arow_s, acol_s, acount_s, brow_s, bcol_s, bcount_s, keep_ref, akey_ref, bkey_ref,
     abuf, lhs, akeys, bkeys, table, table_s, acc, rs1, rs2, colsum, masses,
     local_sem, ring_send, ring_recv, a_send, a_recv, ak_send, ak_recv, bk_send, bk_recv,
     d1_send, d1_recv, d2_send, d2_recv, m_send, m_recv) = scratch[N_ROW:]
    row = lax.axis_index("row")
    col = lax.axis_index("col")
    depth = lax.axis_index("depth")
    y_lo, core = depth // 2, depth % 2
    sibling = y_lo * 2 + (1 - core)
    across = (1 - y_lo) * 2 + core
    across_sibling = (1 - y_lo) * 2 + (1 - core)

    def row_peer(k):
        return lax.rem(row + k, N_ROW)

    def col_peer(k):
        return lax.rem(col + k, N_COL)

    barrier = pltpu.get_barrier_semaphore()
    for k in range(1, N_ROW):
        pl.semaphore_signal(barrier, inc=1, device_id={"row": row_peer(k)}, device_id_type=MESH)
    for k in range(1, N_COL):
        pl.semaphore_signal(barrier, inc=1, device_id={"col": col_peer(k)}, device_id_type=MESH)
    for other in (sibling, across):
        pl.semaphore_signal(barrier, inc=1, device_id={"depth": other}, device_id_type=MESH)

    own_b = pltpu.make_async_copy(b_hbm, tiles[0].at[pl.ds(0, NZB)], local_sem.at[0])
    own_a = pltpu.make_async_copy(a_hbm, abuf.at[col], local_sem.at[1])
    own_keep = pltpu.make_async_copy(keep_hbm, keep_ref, local_sem.at[3])
    pairs = ((arow_hbm, arow_s), (acol_hbm, acol_s), (acount_hbm, acount_s),
             (brow_hbm, brow_s), (bcol_hbm, bcol_s), (bcount_hbm, bcount_s))
    small = [pltpu.make_async_copy(source, target, local_sem.at[4 + i])
             for i, (source, target) in enumerate(pairs)]
    for copy in small + [own_b, own_a, own_keep]:
        copy.start()
    for tile in tiles:
        tile[ABSENT] = jnp.zeros((BS, BS), jnp.bfloat16)
    acc[...] = jnp.zeros_like(acc)
    for copy in small:
        copy.wait()
    lane = lax.broadcasted_iota(jnp.int32, (1, LANES), 1)
    bkey = jnp.full((1, LANES), -1000, jnp.int32)
    for t in range(NZB):
        value = jnp.where(t < bcount_s[0, 0, 0], brow_s[t] * COLB + bcol_s[t], -1000)
        bkey = jnp.where(lane == t, value, bkey)
    akey = jnp.full((1, LANES), -5000, jnp.int32)
    for s in range(NZA):
        value = jnp.where(s < acount_s[0, 0, 0], acol_s[s] * COLB, -5000)
        akey = jnp.where((lane >= s * COLB) & (lane < (s + 1) * COLB), value + lane - s * COLB, akey)
        akey = jnp.where(lane == NZA * COLB + s, arow_s[s], akey)
    akey_ref[...] = akey
    bkey_ref[...] = bkey
    akeys[col] = akey
    bkeys[row] = bkey
    pl.semaphore_wait(barrier, N_ROW - 1 + N_COL - 1 + 2)

    def tile_of(way, step):
        return tiles[step] if way == RIGHT or step == FAR else tiles[FAR + step]

    def hop(way, step, half):
        source = b_hbm if step == 1 else tile_of(way, step - 1)
        part = pl.ds(half * HALF, HALF)
        return pltpu.make_async_remote_copy(
            src_ref=source.at[part],
            dst_ref=tile_of(way, step).at[part],
            send_sem=ring_send.at[way, step, half],
            recv_sem=ring_recv.at[way, step, half],
            device_id={"row": row_peer(1 if way == RIGHT else N_ROW - 1)},
            device_id_type=MESH,
        )

    order = ((RIGHT, 0), (LEFT, 1), (RIGHT, 1), (LEFT, 0))

    def hops(step):
        return order if step < FAR else order[:2]

    def bkey_copy(k):
        return pltpu.make_async_remote_copy(
            src_ref=bkey_ref, dst_ref=bkeys.at[row], send_sem=bk_send.at[k], recv_sem=bk_recv.at[k],
            device_id={"row": row_peer(k)}, device_id_type=MESH)

    def akey_copy(k):
        return pltpu.make_async_remote_copy(
            src_ref=akey_ref, dst_ref=akeys.at[col], send_sem=ak_send.at[k], recv_sem=ak_recv.at[k],
            device_id={"col": col_peer(k)}, device_id_type=MESH)

    def a_copy(k):
        return pltpu.make_async_remote_copy(
            src_ref=a_hbm, dst_ref=abuf.at[col], send_sem=a_send.at[k], recv_sem=a_recv.at[k],
            device_id={"col": col_peer(k)}, device_id_type=MESH)

    for way, half in order:
        hop(way, 1, half).start()
    for k in range(1, N_ROW):
        bkey_copy(k).start()
    for k in range(1, N_COL):
        akey_copy(k).start()
    for k in range(1, N_COL):
        a_copy(k).start()

    own_b.wait()
    own_a.wait()
    own_keep.wait()

    def prepare():
        for k in range(1, N_ROW):
            bkey_copy(k).wait_recv()
        for k in range(1, N_COL):
            akey_copy(k).wait_recv()
        for r in range(N_ROW):
            left = akeys[r // 2]
            wanted = left - (r % 2) * (KBT * COLB)
            have = bkeys[r]
            slot = jnp.full((1, LANES), ABSENT, jnp.int32)
            for t in range(NZB):
                slot = jnp.where(wanted == have[:, t:t + 1], t, slot)
            table[r] = jnp.where(lane < NZA * COLB, slot, left)
        move = pltpu.make_async_copy(table, table_s, local_sem.at[2])
        move.start()
        for k in range(1, N_COL):
            a_copy(k).wait_recv()
        move.wait()

        def stack(c, carry):
            for s in range(NZA):
                block = abuf[c, s]
                which = table_s[2 * c, 0, NZA * COLB + s]
                for i in range(ROWB):
                    lhs[c, i * BS:(i + 1) * BS, s * BS:(s + 1) * BS] = jnp.where(
                        which == i, block, jnp.zeros_like(block))
            return carry

        lax.fori_loop(0, N_COL, stack, 0)

    def multiply(index):
        tile = tiles[index]
        owner = lax.rem(row + (N_ROW - index if index <= FAR else index - FAR), N_ROW)
        left = lhs[owner // 2]

        def part(j, carry):
            strips = []
            for s in range(NZA):
                pair = [tile[table_s[owner, 0, s * COLB + 2 * j + e]] for e in range(2)]
                strips.append(jnp.concatenate(pair, axis=1))
            acc[j] += jnp.dot(left, jnp.concatenate(strips, axis=0), preferred_element_type=jnp.float32)
            return carry

        lax.fori_loop(0, N_DEPTH, part, 0)

    plan = {3: (0, 1, 9), 4: (2, 10, 3), 5: (11, 4, 12), 6: (5, 13), 7: (6, 14), 8: (7, 15)}
    for step in range(2, FAR + 1):
        ahead = hops(step)
        for way, half in order:
            hop(way, step - 1, half).wait_recv()
            if (way, half) in ahead:
                hop(way, step, half).start()
        if step == 3:
            prepare()
        for index in plan.get(step, ()):
            multiply(index)
    for way, half in hops(FAR):
        hop(way, FAR, half).wait_recv()
    multiply(FAR)

    def to_sibling(slot, half):
        part = pl.ds(half * BS, BS)
        which = across_sibling if slot == 0 else sibling
        return pltpu.make_async_remote_copy(
            src_ref=acc.at[which, part], dst_ref=rs1.at[slot, part],
            send_sem=d1_send.at[slot, half], recv_sem=d1_recv.at[slot, half],
            device_id={"depth": sibling}, device_id_type=MESH)

    def to_across(half):
        part = pl.ds(half * BS, BS)
        return pltpu.make_async_remote_copy(
            src_ref=acc.at[across, part], dst_ref=rs2.at[part],
            send_sem=d2_send.at[half], recv_sem=d2_recv.at[half],
            device_id={"depth": across}, device_id_type=MESH)

    for slot in range(2):
        for half in range(ROWB):
            to_sibling(slot, half).start()
    for half in range(ROWB):
        part = pl.ds(half * BS, BS)
        to_sibling(0, half).wait_recv()
        acc[across, part] += rs1[0, part]
        to_across(half).start()
    total = jnp.zeros((1, QUARTER), jnp.float32)
    for half in range(ROWB):
        part = pl.ds(half * BS, BS)
        to_sibling(1, half).wait_recv()
        mine = acc[depth, part] + rs1[1, part]
        to_across(half).wait_recv()
        product = mine + rs2[part]
        pruned = jnp.where(keep_ref[half:half + 1, :] > 0, product, 0.0)
        squares = pruned * pruned
        flow_ref[part] = squares
        total = total + jnp.sum(squares, axis=0, keepdims=True)
    colsum[...] = total
    masses[row] = total

    def mass_copy(k):
        return pltpu.make_async_remote_copy(
            src_ref=colsum, dst_ref=masses.at[row], send_sem=m_send.at[k], recv_sem=m_recv.at[k],
            device_id={"row": row_peer(k)}, device_id_type=MESH)

    for k in range(1, N_ROW):
        mass_copy(k).start()
    for k in range(1, N_ROW):
        mass_copy(k).wait_recv()
    mass = jnp.sum(masses[...], axis=0) * (1.0 / (N_ROW * ROWS)) + epsilon
    flow_ref[...] = flow_ref[...] / mass

    for step in range(1, FAR + 1):
        for way, half in hops(step):
            hop(way, step, half).wait_send()
    for k in range(1, N_ROW):
        bkey_copy(k).wait_send()
        mass_copy(k).wait_send()
    for k in range(1, N_COL):
        akey_copy(k).wait_send()
        a_copy(k).wait_send()
    for half in range(ROWB):
        for slot in range(2):
            to_sibling(slot, half).wait_send()
        to_across(half).wait_send()


def shards(a_vals, a_rows, a_cols, a_count, b_vals, b_rows, b_cols, b_count, keep):
    vmem = pl.BlockSpec(memory_space=pltpu.VMEM)
    hbm = pl.BlockSpec(memory_space=pltpu.HBM)
    dma = pltpu.SemaphoreType.DMA
    return pl.pallas_call(
        kernel,
        out_shape=jax.ShapeDtypeStruct((ROWS, QUARTER), jnp.float32),
        in_specs=[hbm] * 9,
        out_specs=vmem,
        scratch_shapes=[pltpu.VMEM((NZB + 1, BS, BS), jnp.bfloat16)] * N_ROW
        + [
            pltpu.SMEM((NZA,), jnp.int32),
            pltpu.SMEM((NZA,), jnp.int32),
            pltpu.SMEM((1, 1, 1), jnp.int32),
            pltpu.SMEM((NZB,), jnp.int32),
            pltpu.SMEM((NZB,), jnp.int32),
            pltpu.SMEM((1, 1, 1), jnp.int32),
            pltpu.VMEM((ROWB, QUARTER), jnp.int32),
            pltpu.VMEM((1, LANES), jnp.int32),
            pltpu.VMEM((1, LANES), jnp.int32),
            pltpu.VMEM((N_COL, NZA, BS, BS), jnp.bfloat16),
            pltpu.VMEM((N_COL, ROWS, NZA * BS), jnp.bfloat16),
            pltpu.VMEM((N_COL, 1, LANES), jnp.int32),
            pltpu.VMEM((N_ROW, 1, LANES), jnp.int32),
            pltpu.VMEM((N_ROW, 1, LANES), jnp.int32),
            pltpu.SMEM((N_ROW, 1, LANES), jnp.int32),
            pltpu.VMEM((N_DEPTH, ROWS, QUARTER), jnp.float32),
            pltpu.VMEM((2, ROWS, QUARTER), jnp.float32),
            pltpu.VMEM((ROWS, QUARTER), jnp.float32),
            pltpu.VMEM((1, QUARTER), jnp.float32),
            pltpu.VMEM((N_ROW, 1, QUARTER), jnp.float32),
            dma((10,)),
            dma((2, FAR + 1, 2)),
            dma((2, FAR + 1, 2)),
            dma((N_COL,)),
            dma((N_COL,)),
            dma((N_COL,)),
            dma((N_COL,)),
            dma((N_ROW,)),
            dma((N_ROW,)),
            dma((2, ROWB)),
            dma((2, ROWB)),
            dma((ROWB,)),
            dma((ROWB,)),
            dma((N_ROW,)),
            dma((N_ROW,)),
        ],
        compiler_params=pltpu.CompilerParams(
            collective_id=0, has_side_effects=True, vmem_limit_bytes=64 << 20
        ),
    )(
        a_vals.reshape(NZA, BS, BS),
        a_rows.reshape(NZA),
        a_cols.reshape(NZA),
        a_count,
        b_vals.reshape(NZB, BS, BS),
        b_rows.reshape(NZB),
        b_cols.reshape(NZB),
        b_count,
        keep,
    )


def solution(mesh):
    placed = (
        P("row", "depth", "col", None, None, None),
        P("row", "depth", "col", None),
        P("row", "depth", "col", None),
        P("row", "depth", "col"),
        P("depth", "row", "col", None, None, None),
        P("depth", "row", "col", None),
        P("depth", "row", "col", None),
        P("depth", "row", "col"),
        P("row", ("col", "depth")),
    )
    return jax.shard_map(
        shards, mesh=mesh, in_specs=placed, out_specs=P("row", ("col", "depth")), check_vma=False
    )
```

```python
import jax
import jax.numpy as jnp
from jax import lax
from jax.experimental import pallas as pl
from jax.experimental.pallas import tpu as pltpu
from jax.sharding import PartitionSpec as P

BS = 128
ROWB = 2
KT = 32
COLB = 8
KBT = 16
NZA = 4
NZB = 12
N_ROW = 16
N_COL = 8
N_DEPTH = 4
HALF = NZB // 2
FAR = N_ROW // 2
ABSENT = NZB
LANES = 128
QUARTER = COLB * BS // N_DEPTH
ROWS = ROWB * BS
RIGHT, LEFT = 0, 1
PITCH = 16
IDS = N_ROW * PITCH
PER_ROUND = 1
ROUNDS = 26
LAG = 3
OWN = 1
NEAR = OWN + NZB
FRESH = NEAR + 2 * NZB
HELD = FRESH + 2 * ROUNDS * PER_ROUND

epsilon = 1e-06
MESH = pl.DeviceIdType.MESH


def full_ring(a_hbm, arow_hbm, acol_hbm, acount_hbm, b_hbm, brow_hbm, bcol_hbm, bcount_hbm, keep_hbm,
           flow_ref, *scratch):
    tiles = scratch[:N_ROW]
    (arow_s, acol_s, acount_s, brow_s, bcol_s, bcount_s, keep_ref, akey_ref, bkey_ref,
     abuf, lhs, akeys, bkeys, table, table_s, acc, rs1, rs2, colsum, masses,
     local_sem, ring_send, ring_recv, a_send, a_recv, ak_send, ak_recv, bk_send, bk_recv,
     d1_send, d1_recv, d2_send, d2_recv, m_send, m_recv) = scratch[N_ROW:]
    row = lax.axis_index("row")
    col = lax.axis_index("col")
    depth = lax.axis_index("depth")
    y_lo, core = depth // 2, depth % 2
    sibling = y_lo * 2 + (1 - core)
    across = (1 - y_lo) * 2 + core
    across_sibling = (1 - y_lo) * 2 + (1 - core)

    def row_peer(k):
        return lax.rem(row + k, N_ROW)

    def col_peer(k):
        return lax.rem(col + k, N_COL)

    barrier = pltpu.get_barrier_semaphore()
    for k in range(1, N_ROW):
        pl.semaphore_signal(barrier, inc=1, device_id={"row": row_peer(k)}, device_id_type=MESH)
    for k in range(1, N_COL):
        pl.semaphore_signal(barrier, inc=1, device_id={"col": col_peer(k)}, device_id_type=MESH)
    for other in (sibling, across):
        pl.semaphore_signal(barrier, inc=1, device_id={"depth": other}, device_id_type=MESH)

    own_b = pltpu.make_async_copy(b_hbm, tiles[0].at[pl.ds(0, NZB)], local_sem.at[0])
    own_a = pltpu.make_async_copy(a_hbm, abuf.at[col], local_sem.at[1])
    own_keep = pltpu.make_async_copy(keep_hbm, keep_ref, local_sem.at[3])
    pairs = ((arow_hbm, arow_s), (acol_hbm, acol_s), (acount_hbm, acount_s),
             (brow_hbm, brow_s), (bcol_hbm, bcol_s), (bcount_hbm, bcount_s))
    small = [pltpu.make_async_copy(source, target, local_sem.at[4 + i])
             for i, (source, target) in enumerate(pairs)]
    for copy in small + [own_b, own_a, own_keep]:
        copy.start()
    for tile in tiles:
        tile[ABSENT] = jnp.zeros((BS, BS), jnp.bfloat16)
    acc[...] = jnp.zeros_like(acc)
    for copy in small:
        copy.wait()
    lane = lax.broadcasted_iota(jnp.int32, (1, LANES), 1)
    bkey = jnp.full((1, LANES), -1000, jnp.int32)
    for t in range(NZB):
        value = jnp.where(t < bcount_s[0, 0, 0], brow_s[t] * COLB + bcol_s[t], -1000)
        bkey = jnp.where(lane == t, value, bkey)
    akey = jnp.full((1, LANES), -5000, jnp.int32)
    for s in range(NZA):
        value = jnp.where(s < acount_s[0, 0, 0], acol_s[s] * COLB, -5000)
        akey = jnp.where((lane >= s * COLB) & (lane < (s + 1) * COLB), value + lane - s * COLB, akey)
        akey = jnp.where(lane == NZA * COLB + s, arow_s[s], akey)
    akey_ref[...] = akey
    bkey_ref[...] = bkey
    akeys[col] = akey
    bkeys[row] = bkey
    pl.semaphore_wait(barrier, N_ROW - 1 + N_COL - 1 + 2)

    def tile_of(way, step):
        return tiles[step] if way == RIGHT or step == FAR else tiles[FAR + step]

    def hop(way, step, half):
        source = b_hbm if step == 1 else tile_of(way, step - 1)
        part = pl.ds(half * HALF, HALF)
        return pltpu.make_async_remote_copy(
            src_ref=source.at[part],
            dst_ref=tile_of(way, step).at[part],
            send_sem=ring_send.at[way, step, half],
            recv_sem=ring_recv.at[way, step, half],
            device_id={"row": row_peer(1 if way == RIGHT else N_ROW - 1)},
            device_id_type=MESH,
        )

    order = ((RIGHT, 0), (LEFT, 1), (RIGHT, 1), (LEFT, 0))

    def hops(step):
        return order if step < FAR else order[:2]

    def bkey_copy(k):
        return pltpu.make_async_remote_copy(
            src_ref=bkey_ref, dst_ref=bkeys.at[row], send_sem=bk_send.at[k], recv_sem=bk_recv.at[k],
            device_id={"row": row_peer(k)}, device_id_type=MESH)

    def akey_copy(k):
        return pltpu.make_async_remote_copy(
            src_ref=akey_ref, dst_ref=akeys.at[col], send_sem=ak_send.at[k], recv_sem=ak_recv.at[k],
            device_id={"col": col_peer(k)}, device_id_type=MESH)

    def a_copy(k):
        return pltpu.make_async_remote_copy(
            src_ref=a_hbm, dst_ref=abuf.at[col], send_sem=a_send.at[k], recv_sem=a_recv.at[k],
            device_id={"col": col_peer(k)}, device_id_type=MESH)

    for way, half in order:
        hop(way, 1, half).start()
    for k in range(1, N_ROW):
        bkey_copy(k).start()
    for k in range(1, N_COL):
        akey_copy(k).start()
    for k in range(1, N_COL):
        a_copy(k).start()

    own_b.wait()
    own_a.wait()
    own_keep.wait()

    def prepare():
        for k in range(1, N_ROW):
            bkey_copy(k).wait_recv()
        for k in range(1, N_COL):
            akey_copy(k).wait_recv()
        for r in range(N_ROW):
            left = akeys[r // 2]
            wanted = left - (r % 2) * (KBT * COLB)
            have = bkeys[r]
            slot = jnp.full((1, LANES), ABSENT, jnp.int32)
            for t in range(NZB):
                slot = jnp.where(wanted == have[:, t:t + 1], t, slot)
            table[r] = jnp.where(lane < NZA * COLB, slot, left)
        move = pltpu.make_async_copy(table, table_s, local_sem.at[2])
        move.start()
        for k in range(1, N_COL):
            a_copy(k).wait_recv()
        move.wait()

        def stack(c, carry):
            for s in range(NZA):
                block = abuf[c, s]
                which = table_s[2 * c, 0, NZA * COLB + s]
                for i in range(ROWB):
                    lhs[c, i * BS:(i + 1) * BS, s * BS:(s + 1) * BS] = jnp.where(
                        which == i, block, jnp.zeros_like(block))
            return carry

        lax.fori_loop(0, N_COL, stack, 0)

    def multiply(index):
        tile = tiles[index]
        owner = lax.rem(row + (N_ROW - index if index <= FAR else index - FAR), N_ROW)
        left = lhs[owner // 2]

        def part(j, carry):
            strips = []
            for s in range(NZA):
                pair = [tile[table_s[owner, 0, s * COLB + 2 * j + e]] for e in range(2)]
                strips.append(jnp.concatenate(pair, axis=1))
            acc[j] += jnp.dot(left, jnp.concatenate(strips, axis=0), preferred_element_type=jnp.float32)
            return carry

        lax.fori_loop(0, N_DEPTH, part, 0)

    plan = {3: (0, 1, 9), 4: (2, 10, 3), 5: (11, 4, 12), 6: (5, 13), 7: (6, 14), 8: (7, 15)}
    for step in range(2, FAR + 1):
        ahead = hops(step)
        for way, half in order:
            hop(way, step - 1, half).wait_recv()
            if (way, half) in ahead:
                hop(way, step, half).start()
        if step == 3:
            prepare()
        for index in plan.get(step, ()):
            multiply(index)
    for way, half in hops(FAR):
        hop(way, FAR, half).wait_recv()
    multiply(FAR)

    def to_sibling(slot, half):
        part = pl.ds(half * BS, BS)
        which = across_sibling if slot == 0 else sibling
        return pltpu.make_async_remote_copy(
            src_ref=acc.at[which, part], dst_ref=rs1.at[slot, part],
            send_sem=d1_send.at[slot, half], recv_sem=d1_recv.at[slot, half],
            device_id={"depth": sibling}, device_id_type=MESH)

    def to_across(half):
        part = pl.ds(half * BS, BS)
        return pltpu.make_async_remote_copy(
            src_ref=acc.at[across, part], dst_ref=rs2.at[part],
            send_sem=d2_send.at[half], recv_sem=d2_recv.at[half],
            device_id={"depth": across}, device_id_type=MESH)

    for slot in range(2):
        for half in range(ROWB):
            to_sibling(slot, half).start()
    for half in range(ROWB):
        part = pl.ds(half * BS, BS)
        to_sibling(0, half).wait_recv()
        acc[across, part] += rs1[0, part]
        to_across(half).start()
    total = jnp.zeros((1, QUARTER), jnp.float32)
    for half in range(ROWB):
        part = pl.ds(half * BS, BS)
        to_sibling(1, half).wait_recv()
        mine = acc[depth, part] + rs1[1, part]
        to_across(half).wait_recv()
        product = mine + rs2[part]
        pruned = jnp.where(keep_ref[half:half + 1, :] > 0, product, 0.0)
        squares = pruned * pruned
        flow_ref[part] = squares
        total = total + jnp.sum(squares, axis=0, keepdims=True)
    colsum[...] = total
    masses[row] = total

    def mass_copy(k):
        return pltpu.make_async_remote_copy(
            src_ref=colsum, dst_ref=masses.at[row], send_sem=m_send.at[k], recv_sem=m_recv.at[k],
            device_id={"row": row_peer(k)}, device_id_type=MESH)

    for k in range(1, N_ROW):
        mass_copy(k).start()
    for k in range(1, N_ROW):
        mass_copy(k).wait_recv()
    mass = jnp.sum(masses[...], axis=0) * (1.0 / (N_ROW * ROWS)) + epsilon
    flow_ref[...] = flow_ref[...] / mass

    for step in range(1, FAR + 1):
        for way, half in hops(step):
            hop(way, step, half).wait_send()
    for k in range(1, N_ROW):
        bkey_copy(k).wait_send()
        mass_copy(k).wait_send()
    for k in range(1, N_COL):
        akey_copy(k).wait_send()
        a_copy(k).wait_send()
    for half in range(ROWB):
        for slot in range(2):
            to_sibling(slot, half).wait_send()
        to_across(half).wait_send()


def sparse_ring(a_hbm, arow_hbm, acol_hbm, acount_hbm, b_hbm, brow_hbm, bcol_hbm, bcount_hbm, keep_hbm,
                flow_ref, over_ref, *scratch):
    (arow_s, acol_s, acount_s, brow_s, bcol_s, bcount_s, keep_ref, a_note, b_note, need_note,
     abuf, lhs, a_notes, b_notes, needs, table, table_s, plan, plan_s, places, places_s,
     store, stage, landing, flag_note, flags, depth_note, depth_flags,
     acc, rs1, rs2, colsum, masses,
     local_sem, hop_send, hop_recv, round_send, round_recv, a_send, a_recv, an_send, an_recv,
     bn_send, bn_recv, n_send, n_recv, f_send, f_recv, g_send, g_recv,
     d1_send, d1_recv, d2_send, d2_recv, m_send, m_recv) = scratch
    row = lax.axis_index("row")
    col = lax.axis_index("col")
    depth = lax.axis_index("depth")
    y_lo, core = depth // 2, depth % 2
    sibling = y_lo * 2 + (1 - core)
    across = (1 - y_lo) * 2 + core
    across_sibling = (1 - y_lo) * 2 + (1 - core)

    def row_peer(k):
        return lax.rem(row + k, N_ROW)

    def col_peer(k):
        return lax.rem(col + k, N_COL)

    def depth_peer(k):
        return lax.rem(depth + k, N_DEPTH)

    barrier = pltpu.get_barrier_semaphore()
    for k in range(1, N_ROW):
        pl.semaphore_signal(barrier, inc=1, device_id={"row": row_peer(k)}, device_id_type=MESH)
    for k in range(1, N_COL):
        pl.semaphore_signal(barrier, inc=1, device_id={"col": col_peer(k)}, device_id_type=MESH)
    for k in range(1, N_DEPTH):
        pl.semaphore_signal(barrier, inc=1, device_id={"depth": depth_peer(k)}, device_id_type=MESH)

    own_b = pltpu.make_async_copy(b_hbm, store.at[pl.ds(OWN, NZB)], local_sem.at[0])
    own_a = pltpu.make_async_copy(a_hbm, abuf.at[col], local_sem.at[1])
    own_keep = pltpu.make_async_copy(keep_hbm, keep_ref, local_sem.at[3])
    pairs = ((arow_hbm, arow_s), (acol_hbm, acol_s), (acount_hbm, acount_s),
             (brow_hbm, brow_s), (bcol_hbm, bcol_s), (bcount_hbm, bcount_s))
    small = [pltpu.make_async_copy(source, target, local_sem.at[4 + i])
             for i, (source, target) in enumerate(pairs)]
    for copy in small + [own_b, own_a, own_keep]:
        copy.start()
    store[0] = jnp.zeros((BS, BS), jnp.bfloat16)
    acc[...] = jnp.zeros_like(acc)
    for copy in small:
        copy.wait()
    wide = lax.broadcasted_iota(jnp.int32, (1, IDS), 1)
    b_line = jnp.full((1, IDS), -1000, jnp.int32)
    for t in range(NZB):
        value = jnp.where(t < bcount_s[0, 0, 0], brow_s[t] * COLB + bcol_s[t], -1000)
        b_line = jnp.where(wide == row * PITCH + t, value, b_line)
    b_note[...] = b_line
    b_notes[row] = b_line
    here = wide // (2 * PITCH) == col
    odd = (wide // PITCH) % 2
    a_line = jnp.full((1, IDS), -5000, jnp.int32)
    for s in range(NZA):
        value = jnp.where(s < acount_s[0, 0, 0], acol_s[s] * COLB, -5000)
        a_line = jnp.where((wide >= s * COLB) & (wide < (s + 1) * COLB), value + wide - s * COLB, a_line)
        a_line = jnp.where(wide == NZA * COLB + s, arow_s[s], a_line)
        a_note[s:s + 1, :] = jnp.where(here, value - odd * (KBT * COLB), -5000)
    a_note[NZA:, :] = jnp.broadcast_to(a_line, (8 - NZA, IDS))
    a_notes[col] = a_note[...]
    pl.semaphore_wait(barrier, N_ROW - 1 + N_COL - 1 + N_DEPTH - 1)

    def toward(way):
        return {"row": row_peer(1 if way == RIGHT else N_ROW - 1)}

    def hop(way):
        return pltpu.make_async_remote_copy(
            src_ref=b_hbm, dst_ref=store.at[pl.ds(NEAR + way * NZB, NZB)],
            send_sem=hop_send.at[way], recv_sem=hop_recv.at[way],
            device_id=toward(way), device_id_type=MESH)

    def round_copy(way, k):
        return pltpu.make_async_remote_copy(
            src_ref=stage.at[way, k], dst_ref=landing.at[way, k],
            send_sem=round_send.at[way, k], recv_sem=round_recv.at[way, k],
            device_id=toward(way), device_id_type=MESH)

    def b_note_copy(k):
        return pltpu.make_async_remote_copy(
            src_ref=b_note, dst_ref=b_notes.at[row], send_sem=bn_send.at[k], recv_sem=bn_recv.at[k],
            device_id={"row": row_peer(k)}, device_id_type=MESH)

    def need_copy(k):
        return pltpu.make_async_remote_copy(
            src_ref=need_note, dst_ref=needs.at[row], send_sem=n_send.at[k], recv_sem=n_recv.at[k],
            device_id={"row": row_peer(k)}, device_id_type=MESH)

    def a_note_copy(k):
        return pltpu.make_async_remote_copy(
            src_ref=a_note, dst_ref=a_notes.at[col], send_sem=an_send.at[k], recv_sem=an_recv.at[k],
            device_id={"col": col_peer(k)}, device_id_type=MESH)

    def a_copy(k):
        return pltpu.make_async_remote_copy(
            src_ref=a_hbm, dst_ref=abuf.at[col], send_sem=a_send.at[k], recv_sem=a_recv.at[k],
            device_id={"col": col_peer(k)}, device_id_type=MESH)

    def flag_copy(k):
        return pltpu.make_async_remote_copy(
            src_ref=flag_note, dst_ref=flags.at[col], send_sem=f_send.at[k], recv_sem=f_recv.at[k],
            device_id={"col": col_peer(k)}, device_id_type=MESH)

    def depth_flag_copy(k):
        return pltpu.make_async_remote_copy(
            src_ref=depth_note, dst_ref=depth_flags.at[depth], send_sem=g_send.at[k], recv_sem=g_recv.at[k],
            device_id={"depth": depth_peer(k)}, device_id_type=MESH)

    for k in range(1, N_COL):
        a_note_copy(k).start()
    for k in range(1, N_ROW):
        b_note_copy(k).start()

    for k in range(1, N_ROW):
        b_note_copy(k).wait_recv()
    for k in range(1, N_COL):
        a_note_copy(k).wait_recv()
    blocks = b_notes[0]
    for r in range(1, N_ROW):
        blocks = jnp.maximum(blocks, b_notes[r])
    wants = a_notes[0]
    for c in range(1, N_COL):
        wants = jnp.maximum(wants, a_notes[c])
    gap = blocks - wants[:NZA, :]
    hit = jnp.where((gap >= 0) & (gap < COLB), 1, 0)
    need = jnp.max(hit, axis=0, keepdims=True)
    need_note[...] = need
    needs[row] = need
    for k in range(1, N_ROW):
        need_copy(k).start()
    for way in (RIGHT, LEFT):
        hop(way).start()
    for k in range(1, N_COL):
        a_copy(k).start()

    lane = lax.broadcasted_iota(jnp.int32, (1, LANES), 1)
    for c in range(N_COL):
        left = a_notes[c][NZA:NZA + 1, :LANES]
        slot = jnp.full((1, LANES), PITCH - 1, jnp.int32)
        for h in range(2):
            for t in range(NZB):
                at = (2 * c + h) * PITCH + t
                slot = jnp.where(left == blocks[:, at:at + 1] + h * (KBT * COLB), at, slot)
        table[c] = jnp.where(lane < NZA * COLB, slot, left)
    move = pltpu.make_async_copy(table, table_s, local_sem.at[2])
    move.start()

    z = lax.broadcasted_iota(jnp.int32, (N_ROW, IDS), 0)
    ident = lax.broadcasted_iota(jnp.int32, (N_ROW, IDS), 1)
    origin, spot = ident // PITCH, ident % PITCH
    apart = ((z - origin + N_ROW) % N_ROW, (origin - z + N_ROW) % N_ROW)
    reach = (jnp.where(spot < HALF, FAR, FAR - 1), jnp.where(spot < HALF, FAR - 1, FAR))
    for k in range(1, N_ROW):
        need_copy(k).wait_recv()
    wanted = jnp.concatenate([needs[r] for r in range(N_ROW)], axis=0)
    left_to_go, where_at = [], []
    for way in (RIGHT, LEFT):
        inside = (wanted > 0) & (apart[way] >= 1) & (apart[way] <= reach[way])
        last = jnp.max(jnp.where(inside, apart[way], 0), axis=0, keepdims=True)
        left_to_go.append(jnp.where(apart[way] == 1, jnp.maximum(last - 1, 0), 0))
        where_at.append(jnp.where((apart[way] == 1) & (spot < NZB), NEAR + way * NZB + spot, 0))
    slot_of = lax.broadcasted_iota(jnp.int32, (N_ROW, LANES), 1)
    zero_plan = jnp.zeros((N_ROW, LANES), jnp.int32)

    waiting = [jnp.minimum(togo, 0) for togo in left_to_go for _ in range(LAG - 1)]

    def one_round(k, state):
        state = list(state)
        for way in (RIGHT, LEFT):
            togo, at, chosen = state[way], state[2 + way], state[4 + way]
            queue = state[6 + way * (LAG - 1):6 + (way + 1) * (LAG - 1)]
            moved = jnp.zeros_like(togo)
            landed = jnp.zeros_like(togo)
            for m in range(PER_ROUND):
                rank = jnp.where(togo > 0, togo * IDS + ident, 0)
                best = jnp.max(rank, axis=1, keepdims=True)
                pick = (rank == best) & (togo > 0)
                source = jnp.max(jnp.where(pick, at, 0), axis=1, keepdims=True)
                number = k * PER_ROUND + m
                chosen = jnp.where(slot_of == number, source, chosen)
                moved = jnp.where(pick, togo - 1, moved)
                landed = jnp.where(pick, FRESH + way * ROUNDS * PER_ROUND + number, landed)
                togo = jnp.where(pick, 0, togo)
            turn = 1 if way == RIGHT else N_ROW - 1
            queue = [pltpu.roll(moved, turn, 0), *queue]
            state[way] = togo + queue.pop()
            state[6 + way * (LAG - 1):6 + (way + 1) * (LAG - 1)] = queue
            state[2 + way] = jnp.maximum(at, pltpu.roll(landed, turn, 0))
            state[4 + way] = chosen
        return tuple(state)

    state = lax.fori_loop(0, ROUNDS, one_round, (*left_to_go, *where_at, zero_plan, zero_plan, *waiting))
    plan[RIGHT] = state[4]
    plan[LEFT] = state[5]
    plan_move = pltpu.make_async_copy(plan, plan_s, local_sem.at[10])
    plan_move.start()
    own_at = jnp.where((apart[0] == 0) & (spot < NZB), OWN + spot, 0)
    final = jnp.maximum(jnp.maximum(state[2], state[3]), own_at)
    places[0] = final[:, :LANES]
    places[1] = final[:, LANES:]
    places_move = pltpu.make_async_copy(places, places_s, local_sem.at[11])
    places_move.start()
    undone = jnp.maximum(state[0], state[1])
    for late in state[6:]:
        undone = jnp.maximum(undone, late)
    undone = jnp.max(undone, axis=0, keepdims=True)
    undone = jnp.maximum(undone[:, :LANES], undone[:, LANES:])
    flag_note[...] = undone
    flags[col] = undone
    own_b.wait()
    own_a.wait()
    own_keep.wait()
    for way in (RIGHT, LEFT):
        hop(way).wait_recv()
    plan_move.wait()

    def middle(k):
        if k == 0:
            for i in range(1, N_COL):
                flag_copy(i).start()
        if k == 8:
            move.wait()
            for i in range(1, N_COL):
                a_copy(i).wait_recv()

        if 8 <= k < 8 + N_COL:
            for c in (k - 8,):
                for s in range(NZA):
                    block = abuf[c, s]
                    which = table_s[c, 0, NZA * COLB + s]
                    for i in range(ROWB):
                        lhs[c, i * BS:(i + 1) * BS, s * BS:(s + 1) * BS] = jnp.where(
                            which == i, block, jnp.zeros_like(block))
        if k == 18:
            for i in range(1, N_COL):
                flag_copy(i).wait_recv()
            total = flags[0]
            for c in range(1, N_COL):
                total = jnp.maximum(total, flags[c])
            depth_note[...] = total
            depth_flags[depth] = total
            for i in range(1, N_DEPTH):
                depth_flag_copy(i).start()

    for k in range(ROUNDS + LAG):
        for way in (RIGHT, LEFT):
            if k >= LAG:
                round_copy(way, k - LAG).wait_recv()
                for m in range(PER_ROUND):
                    at = FRESH + (way * ROUNDS + k - LAG) * PER_ROUND + m
                    store[at] = landing[way, k - LAG, m]
            if k < ROUNDS:
                for m in range(PER_ROUND):
                    stage[way, k, m] = store[plan_s[way, row, k * PER_ROUND + m]]
                round_copy(way, k).start()
        middle(k)
    places_move.wait()

    def part(j, carry):
        for c in range(N_COL):
            strips = []
            for s in range(NZA):
                pair = []
                for e in range(2):
                    at = table_s[c, 0, s * COLB + 2 * j + e]
                    pair.append(store[places_s[at // LANES, row, at % LANES]])
                strips.append(jnp.concatenate(pair, axis=1))
            acc[j] += jnp.dot(lhs[c], jnp.concatenate(strips, axis=0), preferred_element_type=jnp.float32)
        return carry

    lax.fori_loop(0, N_DEPTH, part, 0)

    def to_sibling(slot, half):
        part = pl.ds(half * BS, BS)
        which = across_sibling if slot == 0 else sibling
        return pltpu.make_async_remote_copy(
            src_ref=acc.at[which, part], dst_ref=rs1.at[slot, part],
            send_sem=d1_send.at[slot, half], recv_sem=d1_recv.at[slot, half],
            device_id={"depth": sibling}, device_id_type=MESH)

    def to_across(half):
        part = pl.ds(half * BS, BS)
        return pltpu.make_async_remote_copy(
            src_ref=acc.at[across, part], dst_ref=rs2.at[part],
            send_sem=d2_send.at[half], recv_sem=d2_recv.at[half],
            device_id={"depth": across}, device_id_type=MESH)

    for slot in range(2):
        for half in range(ROWB):
            to_sibling(slot, half).start()
    for half in range(ROWB):
        part = pl.ds(half * BS, BS)
        to_sibling(0, half).wait_recv()
        acc[across, part] += rs1[0, part]
        to_across(half).start()
    total = jnp.zeros((1, QUARTER), jnp.float32)
    for half in range(ROWB):
        part = pl.ds(half * BS, BS)
        to_sibling(1, half).wait_recv()
        mine = acc[depth, part] + rs1[1, part]
        to_across(half).wait_recv()
        product = mine + rs2[part]
        pruned = jnp.where(keep_ref[half:half + 1, :] > 0, product, 0.0)
        squares = pruned * pruned
        flow_ref[part] = squares
        total = total + jnp.sum(squares, axis=0, keepdims=True)
    colsum[...] = total
    masses[row] = total

    def mass_copy(k):
        return pltpu.make_async_remote_copy(
            src_ref=colsum, dst_ref=masses.at[row], send_sem=m_send.at[k], recv_sem=m_recv.at[k],
            device_id={"row": row_peer(k)}, device_id_type=MESH)

    for k in range(1, N_ROW):
        mass_copy(k).start()
    for k in range(1, N_ROW):
        mass_copy(k).wait_recv()
    mass = jnp.sum(masses[...], axis=0) * (1.0 / (N_ROW * ROWS)) + epsilon
    flow_ref[...] = flow_ref[...] / mass

    for i in range(1, N_DEPTH):
        depth_flag_copy(i).wait_recv()
    over = depth_flags[0]
    for i in range(1, N_DEPTH):
        over = jnp.maximum(over, depth_flags[i])
    over_ref[...] = jnp.broadcast_to(jnp.max(over, axis=1, keepdims=True), (1, LANES))

    for way in (RIGHT, LEFT):
        hop(way).wait_send()
        for k in range(ROUNDS):
            round_copy(way, k).wait_send()
    for k in range(1, N_ROW):
        b_note_copy(k).wait_send()
        need_copy(k).wait_send()
        mass_copy(k).wait_send()
    for k in range(1, N_COL):
        a_note_copy(k).wait_send()
        a_copy(k).wait_send()
        flag_copy(k).wait_send()
    for k in range(1, N_DEPTH):
        depth_flag_copy(k).wait_send()
    for half in range(ROWB):
        for slot in range(2):
            to_sibling(slot, half).wait_send()
        to_across(half).wait_send()


def shards(a_vals, a_rows, a_cols, a_count, b_vals, b_rows, b_cols, b_count, keep):
    vmem = pl.BlockSpec(memory_space=pltpu.VMEM)
    hbm = pl.BlockSpec(memory_space=pltpu.HBM)
    dma = pltpu.SemaphoreType.DMA
    inputs = (
        a_vals.reshape(NZA, BS, BS),
        a_rows.reshape(NZA),
        a_cols.reshape(NZA),
        a_count,
        b_vals.reshape(NZB, BS, BS),
        b_rows.reshape(NZB),
        b_cols.reshape(NZB),
        b_count,
        keep,
    )
    flow = jax.ShapeDtypeStruct((ROWS, QUARTER), jnp.float32)
    words = [
        pltpu.SMEM((NZA,), jnp.int32),
        pltpu.SMEM((NZA,), jnp.int32),
        pltpu.SMEM((1, 1, 1), jnp.int32),
        pltpu.SMEM((NZB,), jnp.int32),
        pltpu.SMEM((NZB,), jnp.int32),
        pltpu.SMEM((1, 1, 1), jnp.int32),
        pltpu.VMEM((ROWB, QUARTER), jnp.int32),
    ]
    sums = [
        pltpu.VMEM((N_DEPTH, ROWS, QUARTER), jnp.float32),
        pltpu.VMEM((2, ROWS, QUARTER), jnp.float32),
        pltpu.VMEM((ROWS, QUARTER), jnp.float32),
        pltpu.VMEM((1, QUARTER), jnp.float32),
        pltpu.VMEM((N_ROW, 1, QUARTER), jnp.float32),
    ]
    tail = [dma((2, ROWB))] * 2 + [dma((ROWB,))] * 2 + [dma((N_ROW,))] * 2
    left = [
        pltpu.VMEM((N_COL, NZA, BS, BS), jnp.bfloat16),
        pltpu.VMEM((N_COL, ROWS, NZA * BS), jnp.bfloat16),
    ]

    def full():
        return pl.pallas_call(
            full_ring,
            out_shape=flow,
            in_specs=[hbm] * 9,
            out_specs=vmem,
            scratch_shapes=[pltpu.VMEM((NZB + 1, BS, BS), jnp.bfloat16)] * N_ROW
            + words
            + [pltpu.VMEM((1, LANES), jnp.int32)] * 2
            + left
            + [
                pltpu.VMEM((N_COL, 1, LANES), jnp.int32),
                pltpu.VMEM((N_ROW, 1, LANES), jnp.int32),
                pltpu.VMEM((N_ROW, 1, LANES), jnp.int32),
                pltpu.SMEM((N_ROW, 1, LANES), jnp.int32),
            ]
            + sums
            + [dma((10,))]
            + [dma((2, FAR + 1, 2))] * 2
            + [dma((N_COL,))] * 4
            + [dma((N_ROW,))] * 2
            + tail,
            compiler_params=pltpu.CompilerParams(
                collective_id=1, has_side_effects=True, vmem_limit_bytes=64 << 20
            ),
        )(*inputs)

    result, over = pl.pallas_call(
        sparse_ring,
        out_shape=(flow, jax.ShapeDtypeStruct((1, LANES), jnp.int32)),
        in_specs=[hbm] * 9,
        out_specs=(vmem, vmem),
        scratch_shapes=words
        + [
            pltpu.VMEM((8, IDS), jnp.int32),
            pltpu.VMEM((1, IDS), jnp.int32),
            pltpu.VMEM((1, IDS), jnp.int32),
        ]
        + left
        + [
            pltpu.VMEM((N_COL, 8, IDS), jnp.int32),
            pltpu.VMEM((N_ROW, 1, IDS), jnp.int32),
            pltpu.VMEM((N_ROW, 1, IDS), jnp.int32),
            pltpu.VMEM((N_COL, 1, LANES), jnp.int32),
            pltpu.SMEM((N_COL, 1, LANES), jnp.int32),
            pltpu.VMEM((2, N_ROW, LANES), jnp.int32),
            pltpu.SMEM((2, N_ROW, LANES), jnp.int32),
            pltpu.VMEM((2, N_ROW, LANES), jnp.int32),
            pltpu.SMEM((2, N_ROW, LANES), jnp.int32),
            pltpu.VMEM((HELD, BS, BS), jnp.bfloat16),
            pltpu.VMEM((2, ROUNDS, PER_ROUND, BS, BS), jnp.bfloat16),
            pltpu.VMEM((2, ROUNDS, PER_ROUND, BS, BS), jnp.bfloat16),
            pltpu.VMEM((1, LANES), jnp.int32),
            pltpu.VMEM((N_COL, 1, LANES), jnp.int32),
            pltpu.VMEM((1, LANES), jnp.int32),
            pltpu.VMEM((N_DEPTH, 1, LANES), jnp.int32),
        ]
        + sums
        + [dma((12,))]
        + [dma((2,))] * 2
        + [dma((2, ROUNDS))] * 2
        + [dma((N_COL,))] * 4
        + [dma((N_ROW,))] * 4
        + [dma((N_COL,))] * 2
        + [dma((N_DEPTH,))] * 2
        + tail,
        compiler_params=pltpu.CompilerParams(
            collective_id=0, has_side_effects=True, vmem_limit_bytes=64 << 20
        ),
    )(*inputs)
    return lax.cond(over[0, 0] > 0, full, lambda: result)


def solution(mesh):
    placed = (
        P("row", "depth", "col", None, None, None),
        P("row", "depth", "col", None),
        P("row", "depth", "col", None),
        P("row", "depth", "col"),
        P("depth", "row", "col", None, None, None),
        P("depth", "row", "col", None),
        P("depth", "row", "col", None),
        P("depth", "row", "col"),
        P("row", ("col", "depth")),
    )
    return jax.shard_map(
        shards, mesh=mesh, in_specs=placed, out_specs=P("row", ("col", "depth")), check_vma=False
    )
```

```python
import jax
import jax.numpy as jnp
from jax import lax
from jax.experimental import pallas as pl
from jax.experimental.pallas import tpu as pltpu
from jax.sharding import PartitionSpec as P

BS = 128
ROWB = 2
KT = 32
COLB = 8
KBT = 16
NZA = 4
NZB = 12
N_ROW = 16
N_COL = 8
N_DEPTH = 4
HALF = NZB // 2
FAR = N_ROW // 2
ABSENT = NZB
LANES = 128
QUARTER = COLB * BS // N_DEPTH
ROWS = ROWB * BS
RIGHT, LEFT = 0, 1
PITCH = 16
IDS = N_ROW * PITCH
PER_ROUND = 1
ROUNDS = 26
LAG = 3
PIECES = (8,) + (2,) * 9
FARTHEST = sorted(range(1, N_ROW), key=lambda k: -min(k, N_ROW - k))
OWN = 1
NEAR = OWN + NZB
FRESH = NEAR + 2 * NZB
HELD = FRESH + 2 * ROUNDS * PER_ROUND

epsilon = 1e-06
MESH = pl.DeviceIdType.MESH


def full_ring(a_hbm, arow_hbm, acol_hbm, acount_hbm, b_hbm, brow_hbm, bcol_hbm, bcount_hbm, keep_hbm,
           flow_ref, *scratch):
    tiles = scratch[:N_ROW]
    (arow_s, acol_s, acount_s, brow_s, bcol_s, bcount_s, keep_ref, akey_ref, bkey_ref,
     abuf, lhs, akeys, bkeys, table, table_s, acc, rs1, rs2, colsum, masses,
     local_sem, ring_send, ring_recv, a_send, a_recv, ak_send, ak_recv, bk_send, bk_recv,
     d1_send, d1_recv, d2_send, d2_recv, m_send, m_recv) = scratch[N_ROW:]
    row = lax.axis_index("row")
    col = lax.axis_index("col")
    depth = lax.axis_index("depth")
    y_lo, core = depth // 2, depth % 2
    sibling = y_lo * 2 + (1 - core)
    across = (1 - y_lo) * 2 + core
    across_sibling = (1 - y_lo) * 2 + (1 - core)

    def row_peer(k):
        return lax.rem(row + k, N_ROW)

    def col_peer(k):
        return lax.rem(col + k, N_COL)

    barrier = pltpu.get_barrier_semaphore()
    for k in range(1, N_ROW):
        pl.semaphore_signal(barrier, inc=1, device_id={"row": row_peer(k)}, device_id_type=MESH)
    for k in range(1, N_COL):
        pl.semaphore_signal(barrier, inc=1, device_id={"col": col_peer(k)}, device_id_type=MESH)
    for other in (sibling, across):
        pl.semaphore_signal(barrier, inc=1, device_id={"depth": other}, device_id_type=MESH)

    own_b = pltpu.make_async_copy(b_hbm, tiles[0].at[pl.ds(0, NZB)], local_sem.at[0])
    own_a = pltpu.make_async_copy(a_hbm, abuf.at[col], local_sem.at[1])
    own_keep = pltpu.make_async_copy(keep_hbm, keep_ref, local_sem.at[3])
    pairs = ((arow_hbm, arow_s), (acol_hbm, acol_s), (acount_hbm, acount_s),
             (brow_hbm, brow_s), (bcol_hbm, bcol_s), (bcount_hbm, bcount_s))
    small = [pltpu.make_async_copy(source, target, local_sem.at[4 + i])
             for i, (source, target) in enumerate(pairs)]
    for copy in small + [own_b, own_a, own_keep]:
        copy.start()
    for tile in tiles:
        tile[ABSENT] = jnp.zeros((BS, BS), jnp.bfloat16)
    acc[...] = jnp.zeros_like(acc)
    for copy in small:
        copy.wait()
    lane = lax.broadcasted_iota(jnp.int32, (1, LANES), 1)
    bkey = jnp.full((1, LANES), -1000, jnp.int32)
    for t in range(NZB):
        value = jnp.where(t < bcount_s[0, 0, 0], brow_s[t] * COLB + bcol_s[t], -1000)
        bkey = jnp.where(lane == t, value, bkey)
    akey = jnp.full((1, LANES), -5000, jnp.int32)
    for s in range(NZA):
        value = jnp.where(s < acount_s[0, 0, 0], acol_s[s] * COLB, -5000)
        akey = jnp.where((lane >= s * COLB) & (lane < (s + 1) * COLB), value + lane - s * COLB, akey)
        akey = jnp.where(lane == NZA * COLB + s, arow_s[s], akey)
    akey_ref[...] = akey
    bkey_ref[...] = bkey
    akeys[col] = akey
    bkeys[row] = bkey
    pl.semaphore_wait(barrier, N_ROW - 1 + N_COL - 1 + 2)

    def tile_of(way, step):
        return tiles[step] if way == RIGHT or step == FAR else tiles[FAR + step]

    def hop(way, step, half):
        source = b_hbm if step == 1 else tile_of(way, step - 1)
        part = pl.ds(half * HALF, HALF)
        return pltpu.make_async_remote_copy(
            src_ref=source.at[part],
            dst_ref=tile_of(way, step).at[part],
            send_sem=ring_send.at[way, step, half],
            recv_sem=ring_recv.at[way, step, half],
            device_id={"row": row_peer(1 if way == RIGHT else N_ROW - 1)},
            device_id_type=MESH,
        )

    order = ((RIGHT, 0), (LEFT, 1), (RIGHT, 1), (LEFT, 0))

    def hops(step):
        return order if step < FAR else order[:2]

    def bkey_copy(k):
        return pltpu.make_async_remote_copy(
            src_ref=bkey_ref, dst_ref=bkeys.at[row], send_sem=bk_send.at[k], recv_sem=bk_recv.at[k],
            device_id={"row": row_peer(k)}, device_id_type=MESH)

    def akey_copy(k):
        return pltpu.make_async_remote_copy(
            src_ref=akey_ref, dst_ref=akeys.at[col], send_sem=ak_send.at[k], recv_sem=ak_recv.at[k],
            device_id={"col": col_peer(k)}, device_id_type=MESH)

    def a_copy(k):
        return pltpu.make_async_remote_copy(
            src_ref=a_hbm, dst_ref=abuf.at[col], send_sem=a_send.at[k], recv_sem=a_recv.at[k],
            device_id={"col": col_peer(k)}, device_id_type=MESH)

    for way, half in order:
        hop(way, 1, half).start()
    for k in range(1, N_ROW):
        bkey_copy(k).start()
    for k in range(1, N_COL):
        akey_copy(k).start()
    for k in range(1, N_COL):
        a_copy(k).start()

    own_b.wait()
    own_a.wait()
    own_keep.wait()

    def prepare():
        for k in range(1, N_ROW):
            bkey_copy(k).wait_recv()
        for k in range(1, N_COL):
            akey_copy(k).wait_recv()
        for r in range(N_ROW):
            left = akeys[r // 2]
            wanted = left - (r % 2) * (KBT * COLB)
            have = bkeys[r]
            slot = jnp.full((1, LANES), ABSENT, jnp.int32)
            for t in range(NZB):
                slot = jnp.where(wanted == have[:, t:t + 1], t, slot)
            table[r] = jnp.where(lane < NZA * COLB, slot, left)
        move = pltpu.make_async_copy(table, table_s, local_sem.at[2])
        move.start()
        for k in range(1, N_COL):
            a_copy(k).wait_recv()
        move.wait()

        def stack(c, carry):
            for s in range(NZA):
                block = abuf[c, s]
                which = table_s[2 * c, 0, NZA * COLB + s]
                for i in range(ROWB):
                    lhs[c, i * BS:(i + 1) * BS, s * BS:(s + 1) * BS] = jnp.where(
                        which == i, block, jnp.zeros_like(block))
            return carry

        lax.fori_loop(0, N_COL, stack, 0)

    def multiply(index):
        tile = tiles[index]
        owner = lax.rem(row + (N_ROW - index if index <= FAR else index - FAR), N_ROW)
        left = lhs[owner // 2]

        def part(j, carry):
            strips = []
            for s in range(NZA):
                pair = [tile[table_s[owner, 0, s * COLB + 2 * j + e]] for e in range(2)]
                strips.append(jnp.concatenate(pair, axis=1))
            acc[j] += jnp.dot(left, jnp.concatenate(strips, axis=0), preferred_element_type=jnp.float32)
            return carry

        lax.fori_loop(0, N_DEPTH, part, 0)

    plan = {3: (0, 1, 9), 4: (2, 10, 3), 5: (11, 4, 12), 6: (5, 13), 7: (6, 14), 8: (7, 15)}
    for step in range(2, FAR + 1):
        ahead = hops(step)
        for way, half in order:
            hop(way, step - 1, half).wait_recv()
            if (way, half) in ahead:
                hop(way, step, half).start()
        if step == 3:
            prepare()
        for index in plan.get(step, ()):
            multiply(index)
    for way, half in hops(FAR):
        hop(way, FAR, half).wait_recv()
    multiply(FAR)

    def to_sibling(slot, half):
        part = pl.ds(half * BS, BS)
        which = across_sibling if slot == 0 else sibling
        return pltpu.make_async_remote_copy(
            src_ref=acc.at[which, part], dst_ref=rs1.at[slot, part],
            send_sem=d1_send.at[slot, half], recv_sem=d1_recv.at[slot, half],
            device_id={"depth": sibling}, device_id_type=MESH)

    def to_across(half):
        part = pl.ds(half * BS, BS)
        return pltpu.make_async_remote_copy(
            src_ref=acc.at[across, part], dst_ref=rs2.at[part],
            send_sem=d2_send.at[half], recv_sem=d2_recv.at[half],
            device_id={"depth": across}, device_id_type=MESH)

    for slot in range(2):
        for half in range(ROWB):
            to_sibling(slot, half).start()
    for half in range(ROWB):
        part = pl.ds(half * BS, BS)
        to_sibling(0, half).wait_recv()
        acc[across, part] += rs1[0, part]
        to_across(half).start()
    total = jnp.zeros((1, QUARTER), jnp.float32)
    for half in range(ROWB):
        part = pl.ds(half * BS, BS)
        to_sibling(1, half).wait_recv()
        mine = acc[depth, part] + rs1[1, part]
        to_across(half).wait_recv()
        product = mine + rs2[part]
        pruned = jnp.where(keep_ref[half:half + 1, :] > 0, product, 0.0)
        squares = pruned * pruned
        flow_ref[part] = squares
        total = total + jnp.sum(squares, axis=0, keepdims=True)
    colsum[...] = total
    masses[row] = total

    def mass_copy(k):
        return pltpu.make_async_remote_copy(
            src_ref=colsum, dst_ref=masses.at[row], send_sem=m_send.at[k], recv_sem=m_recv.at[k],
            device_id={"row": row_peer(k)}, device_id_type=MESH)

    for k in range(1, N_ROW):
        mass_copy(k).start()
    for k in range(1, N_ROW):
        mass_copy(k).wait_recv()
    mass = jnp.sum(masses[...], axis=0) * (1.0 / (N_ROW * ROWS)) + epsilon
    flow_ref[...] = flow_ref[...] / mass

    for step in range(1, FAR + 1):
        for way, half in hops(step):
            hop(way, step, half).wait_send()
    for k in range(1, N_ROW):
        bkey_copy(k).wait_send()
        mass_copy(k).wait_send()
    for k in range(1, N_COL):
        akey_copy(k).wait_send()
        a_copy(k).wait_send()
    for half in range(ROWB):
        for slot in range(2):
            to_sibling(slot, half).wait_send()
        to_across(half).wait_send()


def sparse_ring(a_hbm, arow_hbm, acol_hbm, acount_hbm, b_hbm, brow_hbm, bcol_hbm, bcount_hbm, keep_hbm,
                flow_ref, over_ref, *scratch):
    (arow_s, acol_s, acount_s, brow_s, bcol_s, bcount_s, keep_ref, a_note, b_note, need_note,
     abuf, lhs, a_notes, b_notes, needs, table, table_s, plan, plan_s, places, places_s,
     store, stage, landing, flag_note, flags, depth_note, depth_flags,
     acc, rs1, rs2, colsum, masses,
     local_sem, plan_sem, hop_send, hop_recv, round_send, round_recv, a_send, a_recv, an_send, an_recv,
     bn_send, bn_recv, n_send, n_recv, f_send, f_recv, g_send, g_recv,
     d1_send, d1_recv, d2_send, d2_recv, m_send, m_recv) = scratch
    row = lax.axis_index("row")
    col = lax.axis_index("col")
    depth = lax.axis_index("depth")
    y_lo, core = depth // 2, depth % 2
    sibling = y_lo * 2 + (1 - core)
    across = (1 - y_lo) * 2 + core
    across_sibling = (1 - y_lo) * 2 + (1 - core)

    def row_peer(k):
        return lax.rem(row + k, N_ROW)

    def col_peer(k):
        return lax.rem(col + k, N_COL)

    def depth_peer(k):
        return lax.rem(depth + k, N_DEPTH)

    barrier = pltpu.get_barrier_semaphore()
    for k in range(1, N_ROW):
        pl.semaphore_signal(barrier, inc=1, device_id={"row": row_peer(k)}, device_id_type=MESH)
    for k in range(1, N_COL):
        pl.semaphore_signal(barrier, inc=1, device_id={"col": col_peer(k)}, device_id_type=MESH)
    for k in range(1, N_DEPTH):
        pl.semaphore_signal(barrier, inc=1, device_id={"depth": depth_peer(k)}, device_id_type=MESH)

    own_b = pltpu.make_async_copy(b_hbm, store.at[pl.ds(OWN, NZB)], local_sem.at[0])
    own_a = pltpu.make_async_copy(a_hbm, abuf.at[col], local_sem.at[1])
    own_keep = pltpu.make_async_copy(keep_hbm, keep_ref, local_sem.at[3])
    pairs = ((arow_hbm, arow_s), (acol_hbm, acol_s), (acount_hbm, acount_s),
             (brow_hbm, brow_s), (bcol_hbm, bcol_s), (bcount_hbm, bcount_s))
    small = [pltpu.make_async_copy(source, target, local_sem.at[4 + i])
             for i, (source, target) in enumerate(pairs)]
    for copy in small + [own_b, own_a, own_keep]:
        copy.start()
    store[0] = jnp.zeros((BS, BS), jnp.bfloat16)
    acc[...] = jnp.zeros_like(acc)
    for copy in small:
        copy.wait()
    wide = lax.broadcasted_iota(jnp.int32, (1, IDS), 1)
    b_line = jnp.full((1, IDS), -1000, jnp.int32)
    for t in range(NZB):
        value = jnp.where(t < bcount_s[0, 0, 0], brow_s[t] * COLB + bcol_s[t], -1000)
        b_line = jnp.where(wide == row * PITCH + t, value, b_line)
    b_note[...] = b_line
    b_notes[row] = b_line
    a_rows_line = jnp.zeros((1, IDS), jnp.int32)
    a_line = jnp.full((1, LANES), -5000, jnp.int32)
    lane = lax.broadcasted_iota(jnp.int32, (1, LANES), 1)
    for s in range(NZA):
        live = s < acount_s[0, 0, 0]
        spot_at = jnp.where(live, col * KT + acol_s[s], -1)
        a_rows_line = jnp.where(wide == spot_at, 1, a_rows_line)
        value = jnp.where(live, acol_s[s] * COLB, -5000)
        a_line = jnp.where((lane >= s * COLB) & (lane < (s + 1) * COLB), value + lane - s * COLB, a_line)
        a_line = jnp.where(lane == NZA * COLB + s, arow_s[s], a_line)
    a_note[:, :IDS] = a_rows_line
    a_note[:, IDS:] = a_line
    a_notes[col] = a_note[...]
    pl.semaphore_wait(barrier, N_ROW - 1 + N_COL - 1 + N_DEPTH - 1)

    def toward(way):
        return {"row": row_peer(1 if way == RIGHT else N_ROW - 1)}

    def hop(way):
        return pltpu.make_async_remote_copy(
            src_ref=b_hbm, dst_ref=store.at[pl.ds(NEAR + way * NZB, NZB)],
            send_sem=hop_send.at[way], recv_sem=hop_recv.at[way],
            device_id=toward(way), device_id_type=MESH)

    def round_copy(way, k):
        return pltpu.make_async_remote_copy(
            src_ref=stage.at[way, k], dst_ref=landing.at[way, k],
            send_sem=round_send.at[way, k], recv_sem=round_recv.at[way, k],
            device_id=toward(way), device_id_type=MESH)

    def b_note_copy(k):
        return pltpu.make_async_remote_copy(
            src_ref=b_note, dst_ref=b_notes.at[row], send_sem=bn_send.at[k], recv_sem=bn_recv.at[k],
            device_id={"row": row_peer(k)}, device_id_type=MESH)

    def need_copy(k):
        return pltpu.make_async_remote_copy(
            src_ref=need_note, dst_ref=needs.at[row], send_sem=n_send.at[k], recv_sem=n_recv.at[k],
            device_id={"row": row_peer(k)}, device_id_type=MESH)

    def a_note_copy(k):
        return pltpu.make_async_remote_copy(
            src_ref=a_note, dst_ref=a_notes.at[col], send_sem=an_send.at[k], recv_sem=an_recv.at[k],
            device_id={"col": col_peer(k)}, device_id_type=MESH)

    def a_copy(k):
        return pltpu.make_async_remote_copy(
            src_ref=a_hbm, dst_ref=abuf.at[col], send_sem=a_send.at[k], recv_sem=a_recv.at[k],
            device_id={"col": col_peer(k)}, device_id_type=MESH)

    def flag_copy(k):
        return pltpu.make_async_remote_copy(
            src_ref=flag_note, dst_ref=flags.at[col], send_sem=f_send.at[k], recv_sem=f_recv.at[k],
            device_id={"col": col_peer(k)}, device_id_type=MESH)

    def depth_flag_copy(k):
        return pltpu.make_async_remote_copy(
            src_ref=depth_note, dst_ref=depth_flags.at[depth], send_sem=g_send.at[k], recv_sem=g_recv.at[k],
            device_id={"depth": depth_peer(k)}, device_id_type=MESH)

    for k in range(1, N_COL):
        a_note_copy(k).start()
    for k in FARTHEST:
        b_note_copy(k).start()

    for k in range(1, N_COL):
        a_note_copy(k).wait_recv()
    need = a_notes[0][:, :IDS]
    for c in range(1, N_COL):
        need = jnp.maximum(need, a_notes[c][:, :IDS])
    need_note[...] = need
    needs[row] = need
    for k in FARTHEST:
        need_copy(k).start()
    for way in (RIGHT, LEFT):
        hop(way).start()
    for k in range(1, N_COL):
        a_copy(k).start()

    for k in range(1, N_ROW):
        b_note_copy(k).wait_recv()
    blocks = b_notes[0]
    for r in range(1, N_ROW):
        blocks = jnp.maximum(blocks, b_notes[r])
    inner = jnp.where(blocks >= 0, (wide // PITCH) * KBT + blocks // COLB, -1)
    at_row = lax.broadcasted_iota(jnp.int32, (IDS, IDS), 0)
    spread = jnp.where(at_row == inner, 1.0, 0.0).astype(jnp.bfloat16)
    z = lax.broadcasted_iota(jnp.int32, (N_ROW, IDS), 0)
    ident = lax.broadcasted_iota(jnp.int32, (N_ROW, IDS), 1)
    origin, spot = ident // PITCH, ident % PITCH
    apart = ((z - origin + N_ROW) % N_ROW, (origin - z + N_ROW) % N_ROW)
    reach = (jnp.where(spot < HALF, FAR, FAR - 1), jnp.where(spot < HALF, FAR - 1, FAR))
    for k in range(1, N_ROW):
        need_copy(k).wait_recv()
    asked = jnp.concatenate([needs[r] for r in range(N_ROW)], axis=0)
    wanted = jnp.dot(asked.astype(jnp.float32).astype(jnp.bfloat16), spread, preferred_element_type=jnp.float32)
    left_to_go, where_at = [], []
    for way in (RIGHT, LEFT):
        inside = (wanted > 0.5) & (apart[way] >= 1) & (apart[way] <= reach[way])
        last = jnp.max(jnp.where(inside, apart[way], 0), axis=0, keepdims=True)
        left_to_go.append(jnp.where(apart[way] == 1, jnp.maximum(last - 1, 0), 0))
        where_at.append(jnp.where((apart[way] == 1) & (spot < NZB), NEAR + way * NZB + spot, 0))
    slot_of = lax.broadcasted_iota(jnp.int32, (N_ROW, LANES), 1)
    zero_plan = jnp.zeros((N_ROW, LANES), jnp.int32)

    waiting = [jnp.minimum(togo, 0) for togo in left_to_go for _ in range(LAG - 1)]

    def one_round(k, state):
        state = list(state)
        for way in (RIGHT, LEFT):
            togo, at, chosen = state[way], state[2 + way], state[4 + way]
            queue = state[6 + way * (LAG - 1):6 + (way + 1) * (LAG - 1)]
            moved = jnp.zeros_like(togo)
            landed = jnp.zeros_like(togo)
            for m in range(PER_ROUND):
                rank = jnp.where(togo > 0, togo * IDS + ident, 0)
                best = jnp.max(rank, axis=1, keepdims=True)
                pick = (rank == best) & (togo > 0)
                source = jnp.max(jnp.where(pick, at, 0), axis=1, keepdims=True)
                number = k * PER_ROUND + m
                chosen = jnp.where(slot_of == number, source, chosen)
                moved = jnp.where(pick, togo - 1, moved)
                landed = jnp.where(pick, FRESH + way * ROUNDS * PER_ROUND + number, landed)
                togo = jnp.where(pick, 0, togo)
            turn = 1 if way == RIGHT else N_ROW - 1
            queue = [pltpu.roll(moved, turn, 0), *queue]
            state[way] = togo + queue.pop()
            state[6 + way * (LAG - 1):6 + (way + 1) * (LAG - 1)] = queue
            state[2 + way] = jnp.maximum(at, pltpu.roll(landed, turn, 0))
            state[4 + way] = chosen
        return tuple(state)

    def plan_move(piece):
        return pltpu.make_async_copy(plan.at[piece], plan_s.at[piece], plan_sem.at[piece])

    def schedule(piece, first, last, state):
        state = lax.fori_loop(first, last, one_round, (*state[:4], zero_plan, zero_plan, *state[6:]))
        plan[piece, RIGHT] = state[4]
        plan[piece, LEFT] = state[5]
        plan_move(piece).start()
        return state

    state = schedule(0, 0, PIECES[0], (*left_to_go, *where_at, zero_plan, zero_plan, *waiting))
    own_b.wait()
    own_a.wait()
    own_keep.wait()
    for way in (RIGHT, LEFT):
        hop(way).wait_recv()

    def finish_schedule(state):
        own_at = jnp.where((apart[0] == 0) & (spot < NZB), OWN + spot, 0)
        final = jnp.maximum(jnp.maximum(state[2], state[3]), own_at)
        places[0] = final[:, :LANES]
        places[1] = final[:, LANES:]
        places_move.start()
        undone = jnp.maximum(state[0], state[1])
        for late in state[6:]:
            undone = jnp.maximum(undone, late)
        undone = jnp.max(undone, axis=0, keepdims=True)
        undone = jnp.maximum(undone[:, :LANES], undone[:, LANES:])
        flag_note[...] = undone
        flags[col] = undone
        for i in range(1, N_COL):
            flag_copy(i).start()

    def build_table():
        for c in range(N_COL):
            left = a_notes[c][:, IDS:]
            slot = jnp.full((1, LANES), PITCH - 1, jnp.int32)
            for h in range(2):
                for t in range(NZB):
                    at = (2 * c + h) * PITCH + t
                    slot = jnp.where(left == blocks[:, at:at + 1] + h * (KBT * COLB), at, slot)
            table[c] = jnp.where(lane < NZA * COLB, slot, left)
        move.start()

    def build_left(c):
        for s in range(NZA):
            block = abuf[c, s]
            which = table_s[c, 0, NZA * COLB + s]
            for i in range(ROWB):
                lhs[c, i * BS:(i + 1) * BS, s * BS:(s + 1) * BS] = jnp.where(
                    which == i, block, jnp.zeros_like(block))

    def share_flag():
        for i in range(1, N_COL):
            flag_copy(i).wait_recv()
        total = flags[0]
        for c in range(1, N_COL):
            total = jnp.maximum(total, flags[c])
        depth_note[...] = total
        depth_flags[depth] = total
        for i in range(1, N_DEPTH):
            depth_flag_copy(i).start()

    move = pltpu.make_async_copy(table, table_s, local_sem.at[2])
    places_move = pltpu.make_async_copy(places, places_s, local_sem.at[11])
    piece_of = [p for p, n in enumerate(PIECES) for _ in range(n)]
    starts = [sum(PIECES[:p]) for p in range(len(PIECES))]
    for k in range(ROUNDS + LAG):
        for way in (RIGHT, LEFT):
            if k >= LAG:
                round_copy(way, k - LAG).wait_recv()
                for m in range(PER_ROUND):
                    at = FRESH + (way * ROUNDS + k - LAG) * PER_ROUND + m
                    store[at] = landing[way, k - LAG, m]
            if k < ROUNDS and way == RIGHT and k in starts:
                plan_move(piece_of[k]).wait()
            if k < ROUNDS:
                for m in range(PER_ROUND):
                    stage[way, k, m] = store[plan_s[piece_of[k], way, row, k * PER_ROUND + m]]
                round_copy(way, k).start()
        if k + 1 < len(PIECES):
            state = schedule(k + 1, starts[k + 1], starts[k + 1] + PIECES[k + 1], state)
        if k + 1 == len(PIECES):
            finish_schedule(state)
        if k == len(PIECES):
            build_table()
        if k == len(PIECES) + 2:
            move.wait()
            for i in range(1, N_COL):
                a_copy(i).wait_recv()
        if len(PIECES) + 2 <= k < len(PIECES) + 2 + N_COL:
            build_left(k - len(PIECES) - 2)
        if k == len(PIECES) + 2 + N_COL:
            share_flag()
    places_move.wait()

    def part(j):
        for c in range(N_COL):
            strips = []
            for s in range(NZA):
                pair = []
                for e in range(2):
                    at = table_s[c, 0, s * COLB + 2 * j + e]
                    pair.append(store[places_s[at // LANES, row, at % LANES]])
                strips.append(jnp.concatenate(pair, axis=1))
            acc[j] += jnp.dot(lhs[c], jnp.concatenate(strips, axis=0), preferred_element_type=jnp.float32)


    def to_sibling(slot, half):
        part = pl.ds(half * BS, BS)
        which = across_sibling if slot == 0 else sibling
        return pltpu.make_async_remote_copy(
            src_ref=acc.at[which, part], dst_ref=rs1.at[slot, part],
            send_sem=d1_send.at[slot, half], recv_sem=d1_recv.at[slot, half],
            device_id={"depth": sibling}, device_id_type=MESH)

    def to_across(half):
        part = pl.ds(half * BS, BS)
        return pltpu.make_async_remote_copy(
            src_ref=acc.at[across, part], dst_ref=rs2.at[part],
            send_sem=d2_send.at[half], recv_sem=d2_recv.at[half],
            device_id={"depth": across}, device_id_type=MESH)

    part(across_sibling)
    for half in range(ROWB):
        to_sibling(0, half).start()
    part(across)
    for half in range(ROWB):
        span = pl.ds(half * BS, BS)
        to_sibling(0, half).wait_recv()
        acc[across, span] += rs1[0, span]
        to_across(half).start()
    part(sibling)
    for half in range(ROWB):
        to_sibling(1, half).start()
    part(depth)
    total = jnp.zeros((1, QUARTER), jnp.float32)
    for half in range(ROWB):
        span = pl.ds(half * BS, BS)
        to_sibling(1, half).wait_recv()
        mine = acc[depth, span] + rs1[1, span]
        to_across(half).wait_recv()
        product = mine + rs2[span]
        pruned = jnp.where(keep_ref[half:half + 1, :] > 0, product, 0.0)
        squares = pruned * pruned
        flow_ref[span] = squares
        total = total + jnp.sum(squares, axis=0, keepdims=True)
    colsum[...] = total
    masses[row] = total

    def mass_copy(k):
        return pltpu.make_async_remote_copy(
            src_ref=colsum, dst_ref=masses.at[row], send_sem=m_send.at[k], recv_sem=m_recv.at[k],
            device_id={"row": row_peer(k)}, device_id_type=MESH)

    for k in FARTHEST:
        mass_copy(k).start()
    for k in range(1, N_ROW):
        mass_copy(k).wait_recv()
    mass = jnp.sum(masses[...], axis=0) * (1.0 / (N_ROW * ROWS)) + epsilon
    flow_ref[...] = flow_ref[...] / mass

    for i in range(1, N_DEPTH):
        depth_flag_copy(i).wait_recv()
    over = depth_flags[0]
    for i in range(1, N_DEPTH):
        over = jnp.maximum(over, depth_flags[i])
    over_ref[...] = jnp.broadcast_to(jnp.max(over, axis=1, keepdims=True), (1, LANES))

    for way in (RIGHT, LEFT):
        hop(way).wait_send()
        for k in range(ROUNDS):
            round_copy(way, k).wait_send()
    for k in range(1, N_ROW):
        b_note_copy(k).wait_send()
        need_copy(k).wait_send()
        mass_copy(k).wait_send()
    for k in range(1, N_COL):
        a_note_copy(k).wait_send()
        a_copy(k).wait_send()
        flag_copy(k).wait_send()
    for k in range(1, N_DEPTH):
        depth_flag_copy(k).wait_send()
    for half in range(ROWB):
        for slot in range(2):
            to_sibling(slot, half).wait_send()
        to_across(half).wait_send()


def shards(a_vals, a_rows, a_cols, a_count, b_vals, b_rows, b_cols, b_count, keep):
    vmem = pl.BlockSpec(memory_space=pltpu.VMEM)
    hbm = pl.BlockSpec(memory_space=pltpu.HBM)
    dma = pltpu.SemaphoreType.DMA
    inputs = (
        a_vals.reshape(NZA, BS, BS),
        a_rows.reshape(NZA),
        a_cols.reshape(NZA),
        a_count,
        b_vals.reshape(NZB, BS, BS),
        b_rows.reshape(NZB),
        b_cols.reshape(NZB),
        b_count,
        keep,
    )
    flow = jax.ShapeDtypeStruct((ROWS, QUARTER), jnp.float32)
    words = [
        pltpu.SMEM((NZA,), jnp.int32),
        pltpu.SMEM((NZA,), jnp.int32),
        pltpu.SMEM((1, 1, 1), jnp.int32),
        pltpu.SMEM((NZB,), jnp.int32),
        pltpu.SMEM((NZB,), jnp.int32),
        pltpu.SMEM((1, 1, 1), jnp.int32),
        pltpu.VMEM((ROWB, QUARTER), jnp.int32),
    ]
    sums = [
        pltpu.VMEM((N_DEPTH, ROWS, QUARTER), jnp.float32),
        pltpu.VMEM((2, ROWS, QUARTER), jnp.float32),
        pltpu.VMEM((ROWS, QUARTER), jnp.float32),
        pltpu.VMEM((1, QUARTER), jnp.float32),
        pltpu.VMEM((N_ROW, 1, QUARTER), jnp.float32),
    ]
    tail = [dma((2, ROWB))] * 2 + [dma((ROWB,))] * 2 + [dma((N_ROW,))] * 2
    left = [
        pltpu.VMEM((N_COL, NZA, BS, BS), jnp.bfloat16),
        pltpu.VMEM((N_COL, ROWS, NZA * BS), jnp.bfloat16),
    ]

    def full():
        return pl.pallas_call(
            full_ring,
            out_shape=flow,
            in_specs=[hbm] * 9,
            out_specs=vmem,
            scratch_shapes=[pltpu.VMEM((NZB + 1, BS, BS), jnp.bfloat16)] * N_ROW
            + words
            + [pltpu.VMEM((1, LANES), jnp.int32)] * 2
            + left
            + [
                pltpu.VMEM((N_COL, 1, LANES), jnp.int32),
                pltpu.VMEM((N_ROW, 1, LANES), jnp.int32),
                pltpu.VMEM((N_ROW, 1, LANES), jnp.int32),
                pltpu.SMEM((N_ROW, 1, LANES), jnp.int32),
            ]
            + sums
            + [dma((10,))]
            + [dma((2, FAR + 1, 2))] * 2
            + [dma((N_COL,))] * 4
            + [dma((N_ROW,))] * 2
            + tail,
            compiler_params=pltpu.CompilerParams(
                collective_id=1, has_side_effects=True, vmem_limit_bytes=64 << 20
            ),
        )(*inputs)

    result, over = pl.pallas_call(
        sparse_ring,
        out_shape=(flow, jax.ShapeDtypeStruct((1, LANES), jnp.int32)),
        in_specs=[hbm] * 9,
        out_specs=(vmem, vmem),
        scratch_shapes=words
        + [
            pltpu.VMEM((1, IDS + LANES), jnp.int32),
            pltpu.VMEM((1, IDS), jnp.int32),
            pltpu.VMEM((1, IDS), jnp.int32),
        ]
        + left
        + [
            pltpu.VMEM((N_COL, 1, IDS + LANES), jnp.int32),
            pltpu.VMEM((N_ROW, 1, IDS), jnp.int32),
            pltpu.VMEM((N_ROW, 1, IDS), jnp.int32),
            pltpu.VMEM((N_COL, 1, LANES), jnp.int32),
            pltpu.SMEM((N_COL, 1, LANES), jnp.int32),
            pltpu.VMEM((len(PIECES), 2, N_ROW, LANES), jnp.int32),
            pltpu.SMEM((len(PIECES), 2, N_ROW, LANES), jnp.int32),
            pltpu.VMEM((2, N_ROW, LANES), jnp.int32),
            pltpu.SMEM((2, N_ROW, LANES), jnp.int32),
            pltpu.VMEM((HELD, BS, BS), jnp.bfloat16),
            pltpu.VMEM((2, ROUNDS, PER_ROUND, BS, BS), jnp.bfloat16),
            pltpu.VMEM((2, ROUNDS, PER_ROUND, BS, BS), jnp.bfloat16),
            pltpu.VMEM((1, LANES), jnp.int32),
            pltpu.VMEM((N_COL, 1, LANES), jnp.int32),
            pltpu.VMEM((1, LANES), jnp.int32),
            pltpu.VMEM((N_DEPTH, 1, LANES), jnp.int32),
        ]
        + sums
        + [dma((12,)), dma((len(PIECES),))]
        + [dma((2,))] * 2
        + [dma((2, ROUNDS))] * 2
        + [dma((N_COL,))] * 4
        + [dma((N_ROW,))] * 4
        + [dma((N_COL,))] * 2
        + [dma((N_DEPTH,))] * 2
        + tail,
        compiler_params=pltpu.CompilerParams(
            collective_id=0, has_side_effects=True, vmem_limit_bytes=64 << 20
        ),
    )(*inputs)
    return lax.cond(over[0, 0] > 0, full, lambda: result)


def solution(mesh):
    placed = (
        P("row", "depth", "col", None, None, None),
        P("row", "depth", "col", None),
        P("row", "depth", "col", None),
        P("row", "depth", "col"),
        P("depth", "row", "col", None, None, None),
        P("depth", "row", "col", None),
        P("depth", "row", "col", None),
        P("depth", "row", "col"),
        P("row", ("col", "depth")),
    )
    return jax.shard_map(
        shards, mesh=mesh, in_specs=placed, out_specs=P("row", ("col", "depth")), check_vma=False
    )
```

```python
import jax
import jax.numpy as jnp
from jax import lax
from jax.experimental import pallas as pl
from jax.experimental.pallas import tpu as pltpu
from jax.sharding import PartitionSpec as P

BS = 128
ROWB = 2
KT = 32
COLB = 8
KBT = 16
NZA = 4
NZB = 12
N_ROW = 16
N_COL = 8
N_DEPTH = 4
HALF = NZB // 2
FAR = N_ROW // 2
ABSENT = NZB
LANES = 128
QUARTER = COLB * BS // N_DEPTH
ROWS = ROWB * BS
RIGHT, LEFT = 0, 1
PITCH = 16
IDS = N_ROW * PITCH
PER_ROUND = 1
ROUNDS = 25
LAG = 3
PIECES = (7,) + (2,) * 9
FARTHEST = sorted(range(1, N_ROW), key=lambda k: -min(k, N_ROW - k))
OWN = 1
NEAR = OWN + NZB
FRESH = NEAR + 2 * NZB
HELD = FRESH + 2 * ROUNDS * PER_ROUND

epsilon = 1e-06
MESH = pl.DeviceIdType.MESH


def full_ring(a_hbm, arow_hbm, acol_hbm, acount_hbm, b_hbm, brow_hbm, bcol_hbm, bcount_hbm, keep_hbm,
           flow_ref, *scratch):
    tiles = scratch[:N_ROW]
    (arow_s, acol_s, acount_s, brow_s, bcol_s, bcount_s, keep_ref, akey_ref, bkey_ref,
     abuf, lhs, akeys, bkeys, table, table_s, acc, rs1, rs2, colsum, masses,
     local_sem, ring_send, ring_recv, a_send, a_recv, ak_send, ak_recv, bk_send, bk_recv,
     d1_send, d1_recv, d2_send, d2_recv, m_send, m_recv) = scratch[N_ROW:]
    row = lax.axis_index("row")
    col = lax.axis_index("col")
    depth = lax.axis_index("depth")
    y_lo, core = depth // 2, depth % 2
    sibling = y_lo * 2 + (1 - core)
    across = (1 - y_lo) * 2 + core
    across_sibling = (1 - y_lo) * 2 + (1 - core)

    def row_peer(k):
        return lax.rem(row + k, N_ROW)

    def col_peer(k):
        return lax.rem(col + k, N_COL)

    barrier = pltpu.get_barrier_semaphore()
    for k in range(1, N_ROW):
        pl.semaphore_signal(barrier, inc=1, device_id={"row": row_peer(k)}, device_id_type=MESH)
    for k in range(1, N_COL):
        pl.semaphore_signal(barrier, inc=1, device_id={"col": col_peer(k)}, device_id_type=MESH)
    for other in (sibling, across):
        pl.semaphore_signal(barrier, inc=1, device_id={"depth": other}, device_id_type=MESH)

    own_b = pltpu.make_async_copy(b_hbm, tiles[0].at[pl.ds(0, NZB)], local_sem.at[0])
    own_a = pltpu.make_async_copy(a_hbm, abuf.at[col], local_sem.at[1])
    own_keep = pltpu.make_async_copy(keep_hbm, keep_ref, local_sem.at[3])
    pairs = ((arow_hbm, arow_s), (acol_hbm, acol_s), (acount_hbm, acount_s),
             (brow_hbm, brow_s), (bcol_hbm, bcol_s), (bcount_hbm, bcount_s))
    small = [pltpu.make_async_copy(source, target, local_sem.at[4 + i])
             for i, (source, target) in enumerate(pairs)]
    for copy in small + [own_b, own_a, own_keep]:
        copy.start()
    for tile in tiles:
        tile[ABSENT] = jnp.zeros((BS, BS), jnp.bfloat16)
    acc[...] = jnp.zeros_like(acc)
    for copy in small:
        copy.wait()
    lane = lax.broadcasted_iota(jnp.int32, (1, LANES), 1)
    bkey = jnp.full((1, LANES), -1000, jnp.int32)
    for t in range(NZB):
        value = jnp.where(t < bcount_s[0, 0, 0], brow_s[t] * COLB + bcol_s[t], -1000)
        bkey = jnp.where(lane == t, value, bkey)
    akey = jnp.full((1, LANES), -5000, jnp.int32)
    for s in range(NZA):
        value = jnp.where(s < acount_s[0, 0, 0], acol_s[s] * COLB, -5000)
        akey = jnp.where((lane >= s * COLB) & (lane < (s + 1) * COLB), value + lane - s * COLB, akey)
        akey = jnp.where(lane == NZA * COLB + s, arow_s[s], akey)
    akey_ref[...] = akey
    bkey_ref[...] = bkey
    akeys[col] = akey
    bkeys[row] = bkey
    pl.semaphore_wait(barrier, N_ROW - 1 + N_COL - 1 + 2)

    def tile_of(way, step):
        return tiles[step] if way == RIGHT or step == FAR else tiles[FAR + step]

    def hop(way, step, half):
        source = b_hbm if step == 1 else tile_of(way, step - 1)
        part = pl.ds(half * HALF, HALF)
        return pltpu.make_async_remote_copy(
            src_ref=source.at[part],
            dst_ref=tile_of(way, step).at[part],
            send_sem=ring_send.at[way, step, half],
            recv_sem=ring_recv.at[way, step, half],
            device_id={"row": row_peer(1 if way == RIGHT else N_ROW - 1)},
            device_id_type=MESH,
        )

    order = ((RIGHT, 0), (LEFT, 1), (RIGHT, 1), (LEFT, 0))

    def hops(step):
        return order if step < FAR else order[:2]

    def bkey_copy(k):
        return pltpu.make_async_remote_copy(
            src_ref=bkey_ref, dst_ref=bkeys.at[row], send_sem=bk_send.at[k], recv_sem=bk_recv.at[k],
            device_id={"row": row_peer(k)}, device_id_type=MESH)

    def akey_copy(k):
        return pltpu.make_async_remote_copy(
            src_ref=akey_ref, dst_ref=akeys.at[col], send_sem=ak_send.at[k], recv_sem=ak_recv.at[k],
            device_id={"col": col_peer(k)}, device_id_type=MESH)

    def a_copy(k):
        return pltpu.make_async_remote_copy(
            src_ref=a_hbm, dst_ref=abuf.at[col], send_sem=a_send.at[k], recv_sem=a_recv.at[k],
            device_id={"col": col_peer(k)}, device_id_type=MESH)

    for way, half in order:
        hop(way, 1, half).start()
    for k in range(1, N_ROW):
        bkey_copy(k).start()
    for k in range(1, N_COL):
        akey_copy(k).start()
    for k in range(1, N_COL):
        a_copy(k).start()

    own_b.wait()
    own_a.wait()
    own_keep.wait()

    def prepare():
        for k in range(1, N_ROW):
            bkey_copy(k).wait_recv()
        for k in range(1, N_COL):
            akey_copy(k).wait_recv()
        for r in range(N_ROW):
            left = akeys[r // 2]
            wanted = left - (r % 2) * (KBT * COLB)
            have = bkeys[r]
            slot = jnp.full((1, LANES), ABSENT, jnp.int32)
            for t in range(NZB):
                slot = jnp.where(wanted == have[:, t:t + 1], t, slot)
            table[r] = jnp.where(lane < NZA * COLB, slot, left)
        move = pltpu.make_async_copy(table, table_s, local_sem.at[2])
        move.start()
        for k in range(1, N_COL):
            a_copy(k).wait_recv()
        move.wait()

        def stack(c, carry):
            for s in range(NZA):
                block = abuf[c, s]
                which = table_s[2 * c, 0, NZA * COLB + s]
                for i in range(ROWB):
                    lhs[c, i * BS:(i + 1) * BS, s * BS:(s + 1) * BS] = jnp.where(
                        which == i, block, jnp.zeros_like(block))
            return carry

        lax.fori_loop(0, N_COL, stack, 0)

    def multiply(index):
        tile = tiles[index]
        owner = lax.rem(row + (N_ROW - index if index <= FAR else index - FAR), N_ROW)
        left = lhs[owner // 2]

        def part(j, carry):
            strips = []
            for s in range(NZA):
                pair = [tile[table_s[owner, 0, s * COLB + 2 * j + e]] for e in range(2)]
                strips.append(jnp.concatenate(pair, axis=1))
            acc[j] += jnp.dot(left, jnp.concatenate(strips, axis=0), preferred_element_type=jnp.float32)
            return carry

        lax.fori_loop(0, N_DEPTH, part, 0)

    plan = {3: (0, 1, 9), 4: (2, 10, 3), 5: (11, 4, 12), 6: (5, 13), 7: (6, 14), 8: (7, 15)}
    for step in range(2, FAR + 1):
        ahead = hops(step)
        for way, half in order:
            hop(way, step - 1, half).wait_recv()
            if (way, half) in ahead:
                hop(way, step, half).start()
        if step == 3:
            prepare()
        for index in plan.get(step, ()):
            multiply(index)
    for way, half in hops(FAR):
        hop(way, FAR, half).wait_recv()
    multiply(FAR)

    def to_sibling(slot, half):
        part = pl.ds(half * BS, BS)
        which = across_sibling if slot == 0 else sibling
        return pltpu.make_async_remote_copy(
            src_ref=acc.at[which, part], dst_ref=rs1.at[slot, part],
            send_sem=d1_send.at[slot, half], recv_sem=d1_recv.at[slot, half],
            device_id={"depth": sibling}, device_id_type=MESH)

    def to_across(half):
        part = pl.ds(half * BS, BS)
        return pltpu.make_async_remote_copy(
            src_ref=acc.at[across, part], dst_ref=rs2.at[part],
            send_sem=d2_send.at[half], recv_sem=d2_recv.at[half],
            device_id={"depth": across}, device_id_type=MESH)

    for slot in range(2):
        for half in range(ROWB):
            to_sibling(slot, half).start()
    for half in range(ROWB):
        part = pl.ds(half * BS, BS)
        to_sibling(0, half).wait_recv()
        acc[across, part] += rs1[0, part]
        to_across(half).start()
    total = jnp.zeros((1, QUARTER), jnp.float32)
    for half in range(ROWB):
        part = pl.ds(half * BS, BS)
        to_sibling(1, half).wait_recv()
        mine = acc[depth, part] + rs1[1, part]
        to_across(half).wait_recv()
        product = mine + rs2[part]
        pruned = jnp.where(keep_ref[half:half + 1, :] > 0, product, 0.0)
        squares = pruned * pruned
        flow_ref[part] = squares
        total = total + jnp.sum(squares, axis=0, keepdims=True)
    colsum[...] = total
    masses[row] = total

    def mass_copy(k):
        return pltpu.make_async_remote_copy(
            src_ref=colsum, dst_ref=masses.at[row], send_sem=m_send.at[k], recv_sem=m_recv.at[k],
            device_id={"row": row_peer(k)}, device_id_type=MESH)

    for k in range(1, N_ROW):
        mass_copy(k).start()
    for k in range(1, N_ROW):
        mass_copy(k).wait_recv()
    mass = jnp.sum(masses[...], axis=0) * (1.0 / (N_ROW * ROWS)) + epsilon
    flow_ref[...] = flow_ref[...] / mass

    for step in range(1, FAR + 1):
        for way, half in hops(step):
            hop(way, step, half).wait_send()
    for k in range(1, N_ROW):
        bkey_copy(k).wait_send()
        mass_copy(k).wait_send()
    for k in range(1, N_COL):
        akey_copy(k).wait_send()
        a_copy(k).wait_send()
    for half in range(ROWB):
        for slot in range(2):
            to_sibling(slot, half).wait_send()
        to_across(half).wait_send()


def sparse_ring(a_hbm, arow_hbm, acol_hbm, acount_hbm, b_hbm, brow_hbm, bcol_hbm, bcount_hbm, keep_hbm,
                flow_ref, over_ref, *scratch):
    (arow_s, acol_s, acount_s, brow_s, bcol_s, bcount_s, keep_ref, a_note, b_note, need_note,
     abuf, lhs, a_notes, b_notes, needs, table, table_s, plan, plan_s, places, places_s,
     store, stage, landing, flag_note, flags, depth_note, depth_flags,
     acc, rs1, rs2, colsum, masses,
     local_sem, plan_sem, hop_send, hop_recv, round_send, round_recv, a_send, a_recv, an_send, an_recv,
     bn_send, bn_recv, n_send, n_recv, f_send, f_recv, g_send, g_recv,
     d1_send, d1_recv, d2_send, d2_recv, m_send, m_recv) = scratch
    row = lax.axis_index("row")
    col = lax.axis_index("col")
    depth = lax.axis_index("depth")
    y_lo, core = depth // 2, depth % 2
    sibling = y_lo * 2 + (1 - core)
    across = (1 - y_lo) * 2 + core
    across_sibling = (1 - y_lo) * 2 + (1 - core)

    def row_peer(k):
        return lax.rem(row + k, N_ROW)

    def col_peer(k):
        return lax.rem(col + k, N_COL)

    def depth_peer(k):
        return lax.rem(depth + k, N_DEPTH)

    barrier = pltpu.get_barrier_semaphore()
    for k in range(1, N_ROW):
        pl.semaphore_signal(barrier, inc=1, device_id={"row": row_peer(k)}, device_id_type=MESH)
    for k in range(1, N_COL):
        pl.semaphore_signal(barrier, inc=1, device_id={"col": col_peer(k)}, device_id_type=MESH)
    for k in range(1, N_DEPTH):
        pl.semaphore_signal(barrier, inc=1, device_id={"depth": depth_peer(k)}, device_id_type=MESH)

    own_b = pltpu.make_async_copy(b_hbm, store.at[pl.ds(OWN, NZB)], local_sem.at[0])
    own_a = pltpu.make_async_copy(a_hbm, abuf.at[col], local_sem.at[1])
    own_keep = pltpu.make_async_copy(keep_hbm, keep_ref, local_sem.at[3])
    pairs = ((arow_hbm, arow_s), (acol_hbm, acol_s), (acount_hbm, acount_s),
             (brow_hbm, brow_s), (bcol_hbm, bcol_s), (bcount_hbm, bcount_s))
    small = [pltpu.make_async_copy(source, target, local_sem.at[4 + i])
             for i, (source, target) in enumerate(pairs)]
    for copy in small + [own_b, own_a, own_keep]:
        copy.start()
    store[0] = jnp.zeros((BS, BS), jnp.bfloat16)
    acc[...] = jnp.zeros_like(acc)
    for copy in small:
        copy.wait()
    wide = lax.broadcasted_iota(jnp.int32, (1, IDS), 1)
    b_line = jnp.full((1, IDS), -1000, jnp.int32)
    for t in range(NZB):
        value = jnp.where(t < bcount_s[0, 0, 0], brow_s[t] * COLB + bcol_s[t], -1000)
        b_line = jnp.where(wide == row * PITCH + t, value, b_line)
    b_note[...] = b_line
    b_notes[row] = b_line
    a_rows_line = jnp.zeros((1, IDS), jnp.int32)
    a_line = jnp.full((1, LANES), -5000, jnp.int32)
    lane = lax.broadcasted_iota(jnp.int32, (1, LANES), 1)
    for s in range(NZA):
        live = s < acount_s[0, 0, 0]
        spot_at = jnp.where(live, col * KT + acol_s[s], -1)
        a_rows_line = jnp.where(wide == spot_at, 1, a_rows_line)
        value = jnp.where(live, acol_s[s] * COLB, -5000)
        a_line = jnp.where((lane >= s * COLB) & (lane < (s + 1) * COLB), value + lane - s * COLB, a_line)
        a_line = jnp.where(lane == NZA * COLB + s, arow_s[s], a_line)
    a_note[:, :IDS] = a_rows_line
    a_note[:, IDS:] = a_line
    a_notes[col] = a_note[...]
    pl.semaphore_wait(barrier, N_ROW - 1 + N_COL - 1 + N_DEPTH - 1)

    def toward(way):
        return {"row": row_peer(1 if way == RIGHT else N_ROW - 1)}

    def hop(way):
        return pltpu.make_async_remote_copy(
            src_ref=b_hbm, dst_ref=store.at[pl.ds(NEAR + way * NZB, NZB)],
            send_sem=hop_send.at[way], recv_sem=hop_recv.at[way],
            device_id=toward(way), device_id_type=MESH)

    def round_copy(way, k):
        return pltpu.make_async_remote_copy(
            src_ref=stage.at[way, k], dst_ref=landing.at[way, k],
            send_sem=round_send.at[way, k], recv_sem=round_recv.at[way, k],
            device_id=toward(way), device_id_type=MESH)

    def b_note_copy(k):
        return pltpu.make_async_remote_copy(
            src_ref=b_note, dst_ref=b_notes.at[row], send_sem=bn_send.at[k], recv_sem=bn_recv.at[k],
            device_id={"row": row_peer(k)}, device_id_type=MESH)

    def need_copy(k):
        return pltpu.make_async_remote_copy(
            src_ref=need_note, dst_ref=needs.at[row], send_sem=n_send.at[k], recv_sem=n_recv.at[k],
            device_id={"row": row_peer(k)}, device_id_type=MESH)

    def a_note_copy(k):
        return pltpu.make_async_remote_copy(
            src_ref=a_note, dst_ref=a_notes.at[col], send_sem=an_send.at[k], recv_sem=an_recv.at[k],
            device_id={"col": col_peer(k)}, device_id_type=MESH)

    def a_copy(k):
        return pltpu.make_async_remote_copy(
            src_ref=a_hbm, dst_ref=abuf.at[col], send_sem=a_send.at[k], recv_sem=a_recv.at[k],
            device_id={"col": col_peer(k)}, device_id_type=MESH)

    def flag_copy(k):
        return pltpu.make_async_remote_copy(
            src_ref=flag_note, dst_ref=flags.at[col], send_sem=f_send.at[k], recv_sem=f_recv.at[k],
            device_id={"col": col_peer(k)}, device_id_type=MESH)

    def depth_flag_copy(k):
        return pltpu.make_async_remote_copy(
            src_ref=depth_note, dst_ref=depth_flags.at[depth], send_sem=g_send.at[k], recv_sem=g_recv.at[k],
            device_id={"depth": depth_peer(k)}, device_id_type=MESH)

    for k in range(1, N_COL):
        a_note_copy(k).start()
    for k in FARTHEST:
        b_note_copy(k).start()

    for k in range(1, N_COL):
        a_note_copy(k).wait_recv()
    need = a_notes[0][:, :IDS]
    for c in range(1, N_COL):
        need = jnp.maximum(need, a_notes[c][:, :IDS])
    need_note[...] = need
    needs[row] = need
    for k in FARTHEST:
        need_copy(k).start()
    for way in (RIGHT, LEFT):
        hop(way).start()
    for k in range(1, N_COL):
        a_copy(k).start()

    for k in range(1, N_ROW):
        b_note_copy(k).wait_recv()
    blocks = b_notes[0]
    for r in range(1, N_ROW):
        blocks = jnp.maximum(blocks, b_notes[r])
    inner = jnp.where(blocks >= 0, (wide // PITCH) * KBT + blocks // COLB, -1)
    at_row = lax.broadcasted_iota(jnp.int32, (IDS, IDS), 0)
    spread = jnp.where(at_row == inner, 1.0, 0.0).astype(jnp.bfloat16)
    z = lax.broadcasted_iota(jnp.int32, (N_ROW, IDS), 0)
    ident = lax.broadcasted_iota(jnp.int32, (N_ROW, IDS), 1)
    origin, spot = ident // PITCH, ident % PITCH
    apart = ((z - origin + N_ROW) % N_ROW, (origin - z + N_ROW) % N_ROW)
    reach = (jnp.where(spot < HALF, FAR, FAR - 1), jnp.where(spot < HALF, FAR - 1, FAR))
    for k in range(1, N_ROW):
        need_copy(k).wait_recv()
    asked = jnp.concatenate([needs[r] for r in range(N_ROW)], axis=0)
    wanted = jnp.dot(asked.astype(jnp.float32).astype(jnp.bfloat16), spread, preferred_element_type=jnp.float32)
    left_to_go, where_at = [], []
    for way in (RIGHT, LEFT):
        inside = (wanted > 0.5) & (apart[way] >= 1) & (apart[way] <= reach[way])
        last = jnp.max(jnp.where(inside, apart[way], 0), axis=0, keepdims=True)
        left_to_go.append(jnp.where(apart[way] == 1, jnp.maximum(last - 1, 0), 0))
        where_at.append(jnp.where((apart[way] == 1) & (spot < NZB), NEAR + way * NZB + spot, 0))
    slot_of = lax.broadcasted_iota(jnp.int32, (N_ROW, LANES), 1)
    zero_plan = jnp.zeros((N_ROW, LANES), jnp.int32)

    waiting = [jnp.minimum(togo, 0) for togo in left_to_go for _ in range(LAG - 1)]

    def one_round(k, state):
        state = list(state)
        for way in (RIGHT, LEFT):
            togo, at, chosen = state[way], state[2 + way], state[4 + way]
            queue = state[6 + way * (LAG - 1):6 + (way + 1) * (LAG - 1)]
            moved = jnp.zeros_like(togo)
            landed = jnp.zeros_like(togo)
            for m in range(PER_ROUND):
                rank = jnp.where(togo > 0, togo * IDS + ident, 0)
                best = jnp.max(rank, axis=1, keepdims=True)
                pick = (rank == best) & (togo > 0)
                source = jnp.max(jnp.where(pick, at, 0), axis=1, keepdims=True)
                number = k * PER_ROUND + m
                chosen = jnp.where(slot_of == number, source, chosen)
                moved = jnp.where(pick, togo - 1, moved)
                landed = jnp.where(pick, FRESH + way * ROUNDS * PER_ROUND + number, landed)
                togo = jnp.where(pick, 0, togo)
            turn = 1 if way == RIGHT else N_ROW - 1
            queue = [pltpu.roll(moved, turn, 0), *queue]
            state[way] = togo + queue.pop()
            state[6 + way * (LAG - 1):6 + (way + 1) * (LAG - 1)] = queue
            state[2 + way] = jnp.maximum(at, pltpu.roll(landed, turn, 0))
            state[4 + way] = chosen
        return tuple(state)

    def plan_move(piece):
        return pltpu.make_async_copy(plan.at[piece], plan_s.at[piece], plan_sem.at[piece])

    def schedule(piece, first, last, state):
        state = lax.fori_loop(first, last, one_round, (*state[:4], zero_plan, zero_plan, *state[6:]))
        plan[piece, RIGHT] = state[4]
        plan[piece, LEFT] = state[5]
        plan_move(piece).start()
        return state

    state = schedule(0, 0, PIECES[0], (*left_to_go, *where_at, zero_plan, zero_plan, *waiting))
    own_b.wait()
    own_a.wait()
    own_keep.wait()
    for way in (RIGHT, LEFT):
        hop(way).wait_recv()

    def finish_schedule(state):
        own_at = jnp.where((apart[0] == 0) & (spot < NZB), OWN + spot, 0)
        final = jnp.maximum(jnp.maximum(state[2], state[3]), own_at)
        places[0] = final[:, :LANES]
        places[1] = final[:, LANES:]
        places_move.start()
        undone = jnp.maximum(state[0], state[1])
        for late in state[6:]:
            undone = jnp.maximum(undone, late)
        undone = jnp.max(undone, axis=0, keepdims=True)
        undone = jnp.maximum(undone[:, :LANES], undone[:, LANES:])
        flag_note[...] = undone
        flags[col] = undone
        for i in range(1, N_COL):
            flag_copy(i).start()

    def build_table():
        for c in range(N_COL):
            left = a_notes[c][:, IDS:]
            slot = jnp.full((1, LANES), PITCH - 1, jnp.int32)
            for h in range(2):
                for t in range(NZB):
                    at = (2 * c + h) * PITCH + t
                    slot = jnp.where(left == blocks[:, at:at + 1] + h * (KBT * COLB), at, slot)
            table[c] = jnp.where(lane < NZA * COLB, slot, left)
        move.start()

    def build_left(c):
        for s in range(NZA):
            block = abuf[c, s]
            which = table_s[c, 0, NZA * COLB + s]
            for i in range(ROWB):
                lhs[c, i * BS:(i + 1) * BS, s * BS:(s + 1) * BS] = jnp.where(
                    which == i, block, jnp.zeros_like(block))

    def share_flag():
        for i in range(1, N_COL):
            flag_copy(i).wait_recv()
        total = flags[0]
        for c in range(1, N_COL):
            total = jnp.maximum(total, flags[c])
        depth_note[...] = total
        depth_flags[depth] = total
        for i in range(1, N_DEPTH):
            depth_flag_copy(i).start()

    move = pltpu.make_async_copy(table, table_s, local_sem.at[2])
    places_move = pltpu.make_async_copy(places, places_s, local_sem.at[11])
    piece_of = [p for p, n in enumerate(PIECES) for _ in range(n)]
    starts = [sum(PIECES[:p]) for p in range(len(PIECES))]
    for k in range(ROUNDS + LAG):
        for way in (RIGHT, LEFT):
            if k >= LAG:
                round_copy(way, k - LAG).wait_recv()
                for m in range(PER_ROUND):
                    at = FRESH + (way * ROUNDS + k - LAG) * PER_ROUND + m
                    store[at] = landing[way, k - LAG, m]
            if k < ROUNDS and way == RIGHT and k in starts:
                plan_move(piece_of[k]).wait()
            if k < ROUNDS:
                for m in range(PER_ROUND):
                    stage[way, k, m] = store[plan_s[piece_of[k], way, row, k * PER_ROUND + m]]
                round_copy(way, k).start()
        if k + 1 < len(PIECES):
            state = schedule(k + 1, starts[k + 1], starts[k + 1] + PIECES[k + 1], state)
        if k + 1 == len(PIECES):
            finish_schedule(state)
        if k == len(PIECES):
            build_table()
        if k == len(PIECES) + 2:
            move.wait()
            for i in range(1, N_COL):
                a_copy(i).wait_recv()
        if len(PIECES) + 2 <= k < len(PIECES) + 2 + N_COL:
            build_left(k - len(PIECES) - 2)
        if k == len(PIECES) + 2 + N_COL:
            share_flag()
    places_move.wait()

    def part(j):
        for c in range(N_COL):
            strips = []
            for s in range(NZA):
                pair = []
                for e in range(2):
                    at = table_s[c, 0, s * COLB + 2 * j + e]
                    pair.append(store[places_s[at // LANES, row, at % LANES]])
                strips.append(jnp.concatenate(pair, axis=1))
            acc[j] += jnp.dot(lhs[c], jnp.concatenate(strips, axis=0), preferred_element_type=jnp.float32)


    def to_sibling(slot, half):
        part = pl.ds(half * BS, BS)
        which = across_sibling if slot == 0 else sibling
        return pltpu.make_async_remote_copy(
            src_ref=acc.at[which, part], dst_ref=rs1.at[slot, part],
            send_sem=d1_send.at[slot, half], recv_sem=d1_recv.at[slot, half],
            device_id={"depth": sibling}, device_id_type=MESH)

    def to_across(half):
        part = pl.ds(half * BS, BS)
        return pltpu.make_async_remote_copy(
            src_ref=acc.at[across, part], dst_ref=rs2.at[part],
            send_sem=d2_send.at[half], recv_sem=d2_recv.at[half],
            device_id={"depth": across}, device_id_type=MESH)

    part(across_sibling)
    for half in range(ROWB):
        to_sibling(0, half).start()
    part(across)
    for half in range(ROWB):
        span = pl.ds(half * BS, BS)
        to_sibling(0, half).wait_recv()
        acc[across, span] += rs1[0, span]
        to_across(half).start()
    part(sibling)
    for half in range(ROWB):
        to_sibling(1, half).start()
    part(depth)
    total = jnp.zeros((1, QUARTER), jnp.float32)
    for half in range(ROWB):
        span = pl.ds(half * BS, BS)
        to_sibling(1, half).wait_recv()
        mine = acc[depth, span] + rs1[1, span]
        to_across(half).wait_recv()
        product = mine + rs2[span]
        pruned = jnp.where(keep_ref[half:half + 1, :] > 0, product, 0.0)
        squares = pruned * pruned
        flow_ref[span] = squares
        total = total + jnp.sum(squares, axis=0, keepdims=True)
    colsum[...] = total
    masses[row] = total

    def mass_copy(k):
        return pltpu.make_async_remote_copy(
            src_ref=colsum, dst_ref=masses.at[row], send_sem=m_send.at[k], recv_sem=m_recv.at[k],
            device_id={"row": row_peer(k)}, device_id_type=MESH)

    for k in FARTHEST:
        mass_copy(k).start()
    for k in range(1, N_ROW):
        mass_copy(k).wait_recv()
    mass = jnp.sum(masses[...], axis=0) * (1.0 / (N_ROW * ROWS)) + epsilon
    flow_ref[...] = flow_ref[...] / mass

    for i in range(1, N_DEPTH):
        depth_flag_copy(i).wait_recv()
    over = depth_flags[0]
    for i in range(1, N_DEPTH):
        over = jnp.maximum(over, depth_flags[i])
    over_ref[0, 0] = jnp.max(over)

    for way in (RIGHT, LEFT):
        hop(way).wait_send()
        for k in range(ROUNDS):
            round_copy(way, k).wait_send()
    for k in range(1, N_ROW):
        b_note_copy(k).wait_send()
        need_copy(k).wait_send()
        mass_copy(k).wait_send()
    for k in range(1, N_COL):
        a_note_copy(k).wait_send()
        a_copy(k).wait_send()
        flag_copy(k).wait_send()
    for k in range(1, N_DEPTH):
        depth_flag_copy(k).wait_send()
    for half in range(ROWB):
        for slot in range(2):
            to_sibling(slot, half).wait_send()
        to_across(half).wait_send()


def shards(a_vals, a_rows, a_cols, a_count, b_vals, b_rows, b_cols, b_count, keep):
    vmem = pl.BlockSpec(memory_space=pltpu.VMEM)
    hbm = pl.BlockSpec(memory_space=pltpu.HBM)
    dma = pltpu.SemaphoreType.DMA
    inputs = (
        a_vals.reshape(NZA, BS, BS),
        a_rows.reshape(NZA),
        a_cols.reshape(NZA),
        a_count,
        b_vals.reshape(NZB, BS, BS),
        b_rows.reshape(NZB),
        b_cols.reshape(NZB),
        b_count,
        keep,
    )
    flow = jax.ShapeDtypeStruct((ROWS, QUARTER), jnp.float32)
    words = [
        pltpu.SMEM((NZA,), jnp.int32),
        pltpu.SMEM((NZA,), jnp.int32),
        pltpu.SMEM((1, 1, 1), jnp.int32),
        pltpu.SMEM((NZB,), jnp.int32),
        pltpu.SMEM((NZB,), jnp.int32),
        pltpu.SMEM((1, 1, 1), jnp.int32),
        pltpu.VMEM((ROWB, QUARTER), jnp.int32),
    ]
    sums = [
        pltpu.VMEM((N_DEPTH, ROWS, QUARTER), jnp.float32),
        pltpu.VMEM((2, ROWS, QUARTER), jnp.float32),
        pltpu.VMEM((ROWS, QUARTER), jnp.float32),
        pltpu.VMEM((1, QUARTER), jnp.float32),
        pltpu.VMEM((N_ROW, 1, QUARTER), jnp.float32),
    ]
    tail = [dma((2, ROWB))] * 2 + [dma((ROWB,))] * 2 + [dma((N_ROW,))] * 2
    left = [
        pltpu.VMEM((N_COL, NZA, BS, BS), jnp.bfloat16),
        pltpu.VMEM((N_COL, ROWS, NZA * BS), jnp.bfloat16),
    ]

    def full():
        return pl.pallas_call(
            full_ring,
            out_shape=flow,
            in_specs=[hbm] * 9,
            out_specs=vmem,
            scratch_shapes=[pltpu.VMEM((NZB + 1, BS, BS), jnp.bfloat16)] * N_ROW
            + words
            + [pltpu.VMEM((1, LANES), jnp.int32)] * 2
            + left
            + [
                pltpu.VMEM((N_COL, 1, LANES), jnp.int32),
                pltpu.VMEM((N_ROW, 1, LANES), jnp.int32),
                pltpu.VMEM((N_ROW, 1, LANES), jnp.int32),
                pltpu.SMEM((N_ROW, 1, LANES), jnp.int32),
            ]
            + sums
            + [dma((10,))]
            + [dma((2, FAR + 1, 2))] * 2
            + [dma((N_COL,))] * 4
            + [dma((N_ROW,))] * 2
            + tail,
            compiler_params=pltpu.CompilerParams(
                collective_id=1, has_side_effects=True, vmem_limit_bytes=64 << 20
            ),
        )(*inputs)

    result, over = pl.pallas_call(
        sparse_ring,
        out_shape=(flow, jax.ShapeDtypeStruct((1, 1), jnp.int32)),
        in_specs=[hbm] * 9,
        out_specs=(vmem, pl.BlockSpec(memory_space=pltpu.SMEM)),
        scratch_shapes=words
        + [
            pltpu.VMEM((1, IDS + LANES), jnp.int32),
            pltpu.VMEM((1, IDS), jnp.int32),
            pltpu.VMEM((1, IDS), jnp.int32),
        ]
        + left
        + [
            pltpu.VMEM((N_COL, 1, IDS + LANES), jnp.int32),
            pltpu.VMEM((N_ROW, 1, IDS), jnp.int32),
            pltpu.VMEM((N_ROW, 1, IDS), jnp.int32),
            pltpu.VMEM((N_COL, 1, LANES), jnp.int32),
            pltpu.SMEM((N_COL, 1, LANES), jnp.int32),
            pltpu.VMEM((len(PIECES), 2, N_ROW, LANES), jnp.int32),
            pltpu.SMEM((len(PIECES), 2, N_ROW, LANES), jnp.int32),
            pltpu.VMEM((2, N_ROW, LANES), jnp.int32),
            pltpu.SMEM((2, N_ROW, LANES), jnp.int32),
            pltpu.VMEM((HELD, BS, BS), jnp.bfloat16),
            pltpu.VMEM((2, ROUNDS, PER_ROUND, BS, BS), jnp.bfloat16),
            pltpu.VMEM((2, ROUNDS, PER_ROUND, BS, BS), jnp.bfloat16),
            pltpu.VMEM((1, LANES), jnp.int32),
            pltpu.VMEM((N_COL, 1, LANES), jnp.int32),
            pltpu.VMEM((1, LANES), jnp.int32),
            pltpu.VMEM((N_DEPTH, 1, LANES), jnp.int32),
        ]
        + sums
        + [dma((12,)), dma((len(PIECES),))]
        + [dma((2,))] * 2
        + [dma((2, ROUNDS))] * 2
        + [dma((N_COL,))] * 4
        + [dma((N_ROW,))] * 4
        + [dma((N_COL,))] * 2
        + [dma((N_DEPTH,))] * 2
        + tail,
        compiler_params=pltpu.CompilerParams(
            collective_id=0, has_side_effects=True, vmem_limit_bytes=64 << 20
        ),
    )(*inputs)
    return lax.cond(over[0, 0] > 0, full, lambda: result)


def solution(mesh):
    placed = (
        P("row", "depth", "col", None, None, None),
        P("row", "depth", "col", None),
        P("row", "depth", "col", None),
        P("row", "depth", "col"),
        P("depth", "row", "col", None, None, None),
        P("depth", "row", "col", None),
        P("depth", "row", "col", None),
        P("depth", "row", "col"),
        P("row", ("col", "depth")),
    )
    return jax.shard_map(
        shards, mesh=mesh, in_specs=placed, out_specs=P("row", ("col", "depth")), check_vma=False
    )
```

```python
import jax
import jax.numpy as jnp
from jax import lax
from jax.experimental import pallas as pl
from jax.experimental.pallas import tpu as pltpu
from jax.sharding import PartitionSpec as P

BS = 128
ROWB = 2
KT = 32
COLB = 8
KBT = 16
NZA = 4
NZB = 12
N_ROW = 16
N_COL = 8
N_DEPTH = 4
HALF = NZB // 2
FAR = N_ROW // 2
ABSENT = NZB
LANES = 128
QUARTER = COLB * BS // N_DEPTH
ROWS = ROWB * BS
RIGHT, LEFT = 0, 1
PITCH = 16
IDS = N_ROW * PITCH
PER_ROUND = 1
ROUNDS = 25
LAG = 3
PIECES = (7,) + (2,) * 9
FARTHEST = sorted(range(1, N_ROW), key=lambda k: -min(k, N_ROW - k))
OWN = 1
NEAR = OWN + NZB
FRESH = NEAR + 2 * NZB
HELD = FRESH + 2 * ROUNDS * PER_ROUND

epsilon = 1e-06
MESH = pl.DeviceIdType.MESH


def full_ring(a_hbm, arow_hbm, acol_hbm, acount_hbm, b_hbm, brow_hbm, bcol_hbm, bcount_hbm, keep_hbm,
           flow_ref, *scratch):
    tiles = scratch[:N_ROW]
    (arow_s, acol_s, acount_s, brow_s, bcol_s, bcount_s, keep_ref, akey_ref, bkey_ref,
     abuf, lhs, akeys, bkeys, table, table_s, acc, rs1, rs2, colsum, masses,
     local_sem, ring_send, ring_recv, a_send, a_recv, ak_send, ak_recv, bk_send, bk_recv,
     d1_send, d1_recv, d2_send, d2_recv, m_send, m_recv) = scratch[N_ROW:]
    row = lax.axis_index("row")
    col = lax.axis_index("col")
    depth = lax.axis_index("depth")
    y_lo, core = depth // 2, depth % 2
    sibling = y_lo * 2 + (1 - core)
    across = (1 - y_lo) * 2 + core
    across_sibling = (1 - y_lo) * 2 + (1 - core)

    def row_peer(k):
        return lax.rem(row + k, N_ROW)

    def col_peer(k):
        return lax.rem(col + k, N_COL)

    barrier = pltpu.get_barrier_semaphore()
    for k in range(1, N_ROW):
        pl.semaphore_signal(barrier, inc=1, device_id={"row": row_peer(k)}, device_id_type=MESH)
    for k in range(1, N_COL):
        pl.semaphore_signal(barrier, inc=1, device_id={"col": col_peer(k)}, device_id_type=MESH)
    for other in (sibling, across):
        pl.semaphore_signal(barrier, inc=1, device_id={"depth": other}, device_id_type=MESH)

    own_b = pltpu.make_async_copy(b_hbm, tiles[0].at[pl.ds(0, NZB)], local_sem.at[0])
    own_a = pltpu.make_async_copy(a_hbm, abuf.at[col], local_sem.at[1])
    own_keep = pltpu.make_async_copy(keep_hbm, keep_ref, local_sem.at[3])
    pairs = ((arow_hbm, arow_s), (acol_hbm, acol_s), (acount_hbm, acount_s),
             (brow_hbm, brow_s), (bcol_hbm, bcol_s), (bcount_hbm, bcount_s))
    small = [pltpu.make_async_copy(source, target, local_sem.at[4 + i])
             for i, (source, target) in enumerate(pairs)]
    for copy in small + [own_b, own_a, own_keep]:
        copy.start()
    for tile in tiles:
        tile[ABSENT] = jnp.zeros((BS, BS), jnp.bfloat16)
    acc[...] = jnp.zeros_like(acc)
    for copy in small:
        copy.wait()
    lane = lax.broadcasted_iota(jnp.int32, (1, LANES), 1)
    bkey = jnp.full((1, LANES), -1000, jnp.int32)
    for t in range(NZB):
        value = jnp.where(t < bcount_s[0, 0, 0], brow_s[t] * COLB + bcol_s[t], -1000)
        bkey = jnp.where(lane == t, value, bkey)
    akey = jnp.full((1, LANES), -5000, jnp.int32)
    for s in range(NZA):
        value = jnp.where(s < acount_s[0, 0, 0], acol_s[s] * COLB, -5000)
        akey = jnp.where((lane >= s * COLB) & (lane < (s + 1) * COLB), value + lane - s * COLB, akey)
        akey = jnp.where(lane == NZA * COLB + s, arow_s[s], akey)
    akey_ref[...] = akey
    bkey_ref[...] = bkey
    akeys[col] = akey
    bkeys[row] = bkey
    pl.semaphore_wait(barrier, N_ROW - 1 + N_COL - 1 + 2)

    def tile_of(way, step):
        return tiles[step] if way == RIGHT or step == FAR else tiles[FAR + step]

    def hop(way, step, half):
        source = b_hbm if step == 1 else tile_of(way, step - 1)
        part = pl.ds(half * HALF, HALF)
        return pltpu.make_async_remote_copy(
            src_ref=source.at[part],
            dst_ref=tile_of(way, step).at[part],
            send_sem=ring_send.at[way, step, half],
            recv_sem=ring_recv.at[way, step, half],
            device_id={"row": row_peer(1 if way == RIGHT else N_ROW - 1)},
            device_id_type=MESH,
        )

    order = ((RIGHT, 0), (LEFT, 1), (RIGHT, 1), (LEFT, 0))

    def hops(step):
        return order if step < FAR else order[:2]

    def bkey_copy(k):
        return pltpu.make_async_remote_copy(
            src_ref=bkey_ref, dst_ref=bkeys.at[row], send_sem=bk_send.at[k], recv_sem=bk_recv.at[k],
            device_id={"row": row_peer(k)}, device_id_type=MESH)

    def akey_copy(k):
        return pltpu.make_async_remote_copy(
            src_ref=akey_ref, dst_ref=akeys.at[col], send_sem=ak_send.at[k], recv_sem=ak_recv.at[k],
            device_id={"col": col_peer(k)}, device_id_type=MESH)

    def a_copy(k):
        return pltpu.make_async_remote_copy(
            src_ref=a_hbm, dst_ref=abuf.at[col], send_sem=a_send.at[k], recv_sem=a_recv.at[k],
            device_id={"col": col_peer(k)}, device_id_type=MESH)

    for way, half in order:
        hop(way, 1, half).start()
    for k in range(1, N_ROW):
        bkey_copy(k).start()
    for k in range(1, N_COL):
        akey_copy(k).start()
    for k in range(1, N_COL):
        a_copy(k).start()

    own_b.wait()
    own_a.wait()
    own_keep.wait()

    def prepare():
        for k in range(1, N_ROW):
            bkey_copy(k).wait_recv()
        for k in range(1, N_COL):
            akey_copy(k).wait_recv()
        for r in range(N_ROW):
            left = akeys[r // 2]
            wanted = left - (r % 2) * (KBT * COLB)
            have = bkeys[r]
            slot = jnp.full((1, LANES), ABSENT, jnp.int32)
            for t in range(NZB):
                slot = jnp.where(wanted == have[:, t:t + 1], t, slot)
            table[r] = jnp.where(lane < NZA * COLB, slot, left)
        move = pltpu.make_async_copy(table, table_s, local_sem.at[2])
        move.start()
        for k in range(1, N_COL):
            a_copy(k).wait_recv()
        move.wait()

        def stack(c, carry):
            for s in range(NZA):
                block = abuf[c, s]
                which = table_s[2 * c, 0, NZA * COLB + s]
                for i in range(ROWB):
                    lhs[c, i * BS:(i + 1) * BS, s * BS:(s + 1) * BS] = jnp.where(
                        which == i, block, jnp.zeros_like(block))
            return carry

        lax.fori_loop(0, N_COL, stack, 0)

    def multiply(index):
        tile = tiles[index]
        owner = lax.rem(row + (N_ROW - index if index <= FAR else index - FAR), N_ROW)
        left = lhs[owner // 2]

        def part(j, carry):
            strips = []
            for s in range(NZA):
                pair = [tile[table_s[owner, 0, s * COLB + 2 * j + e]] for e in range(2)]
                strips.append(jnp.concatenate(pair, axis=1))
            acc[j] += jnp.dot(left, jnp.concatenate(strips, axis=0), preferred_element_type=jnp.float32)
            return carry

        lax.fori_loop(0, N_DEPTH, part, 0)

    plan = {3: (0, 1, 9), 4: (2, 10, 3), 5: (11, 4, 12), 6: (5, 13), 7: (6, 14), 8: (7, 15)}
    for step in range(2, FAR + 1):
        ahead = hops(step)
        for way, half in order:
            hop(way, step - 1, half).wait_recv()
            if (way, half) in ahead:
                hop(way, step, half).start()
        if step == 3:
            prepare()
        for index in plan.get(step, ()):
            multiply(index)
    for way, half in hops(FAR):
        hop(way, FAR, half).wait_recv()
    multiply(FAR)

    def to_sibling(slot, half):
        part = pl.ds(half * BS, BS)
        which = across_sibling if slot == 0 else sibling
        return pltpu.make_async_remote_copy(
            src_ref=acc.at[which, part], dst_ref=rs1.at[slot, part],
            send_sem=d1_send.at[slot, half], recv_sem=d1_recv.at[slot, half],
            device_id={"depth": sibling}, device_id_type=MESH)

    def to_across(half):
        part = pl.ds(half * BS, BS)
        return pltpu.make_async_remote_copy(
            src_ref=acc.at[across, part], dst_ref=rs2.at[part],
            send_sem=d2_send.at[half], recv_sem=d2_recv.at[half],
            device_id={"depth": across}, device_id_type=MESH)

    for slot in range(2):
        for half in range(ROWB):
            to_sibling(slot, half).start()
    for half in range(ROWB):
        part = pl.ds(half * BS, BS)
        to_sibling(0, half).wait_recv()
        acc[across, part] += rs1[0, part]
        to_across(half).start()
    total = jnp.zeros((1, QUARTER), jnp.float32)
    for half in range(ROWB):
        part = pl.ds(half * BS, BS)
        to_sibling(1, half).wait_recv()
        mine = acc[depth, part] + rs1[1, part]
        to_across(half).wait_recv()
        product = mine + rs2[part]
        pruned = jnp.where(keep_ref[half:half + 1, :] > 0, product, 0.0)
        squares = pruned * pruned
        flow_ref[part] = squares
        total = total + jnp.sum(squares, axis=0, keepdims=True)
    colsum[...] = total
    masses[row] = total

    def mass_copy(k):
        return pltpu.make_async_remote_copy(
            src_ref=colsum, dst_ref=masses.at[row], send_sem=m_send.at[k], recv_sem=m_recv.at[k],
            device_id={"row": row_peer(k)}, device_id_type=MESH)

    for k in range(1, N_ROW):
        mass_copy(k).start()
    for k in range(1, N_ROW):
        mass_copy(k).wait_recv()
    mass = jnp.sum(masses[...], axis=0) * (1.0 / (N_ROW * ROWS)) + epsilon
    flow_ref[...] = flow_ref[...] / mass

    for step in range(1, FAR + 1):
        for way, half in hops(step):
            hop(way, step, half).wait_send()
    for k in range(1, N_ROW):
        bkey_copy(k).wait_send()
        mass_copy(k).wait_send()
    for k in range(1, N_COL):
        akey_copy(k).wait_send()
        a_copy(k).wait_send()
    for half in range(ROWB):
        for slot in range(2):
            to_sibling(slot, half).wait_send()
        to_across(half).wait_send()


def sparse_ring(a_hbm, arow_hbm, acol_hbm, acount_hbm, b_hbm, brow_hbm, bcol_hbm, bcount_hbm, keep_hbm,
                flow_ref, over_ref, *scratch):
    (arow_s, acol_s, acount_s, brow_s, bcol_s, bcount_s, keep_ref, a_note, b_note, need_note,
     abuf, lhs, a_notes, b_notes, needs, table, table_s, plan, plan_s, places, places_s,
     store, stage, landing, flag_note, flags, depth_note, depth_flags,
     acc, rs1, rs2, colsum, masses,
     local_sem, plan_sem, hop_send, hop_recv, round_send, round_recv, a_send, a_recv, an_send, an_recv,
     bn_send, bn_recv, n_send, n_recv, f_send, f_recv, g_send, g_recv,
     d1_send, d1_recv, d2_send, d2_recv, m_send, m_recv) = scratch
    row = lax.axis_index("row")
    col = lax.axis_index("col")
    depth = lax.axis_index("depth")
    y_lo, core = depth // 2, depth % 2
    sibling = y_lo * 2 + (1 - core)
    across = (1 - y_lo) * 2 + core
    across_sibling = (1 - y_lo) * 2 + (1 - core)

    def row_peer(k):
        return lax.rem(row + k, N_ROW)

    def col_peer(k):
        return lax.rem(col + k, N_COL)

    def depth_peer(k):
        return lax.rem(depth + k, N_DEPTH)

    barrier = pltpu.get_barrier_semaphore()
    for k in FARTHEST:
        pl.semaphore_signal(barrier, inc=1, device_id={"row": row_peer(k)}, device_id_type=MESH)
    for k in range(1, N_COL):
        pl.semaphore_signal(barrier, inc=1, device_id={"col": col_peer(k)}, device_id_type=MESH)
    for k in range(1, N_DEPTH):
        pl.semaphore_signal(barrier, inc=1, device_id={"depth": depth_peer(k)}, device_id_type=MESH)

    own_b = pltpu.make_async_copy(b_hbm, store.at[pl.ds(OWN, NZB)], local_sem.at[0])
    own_a = pltpu.make_async_copy(a_hbm, abuf.at[col], local_sem.at[1])
    own_keep = pltpu.make_async_copy(keep_hbm, keep_ref, local_sem.at[3])
    pairs = ((arow_hbm, arow_s), (acol_hbm, acol_s), (acount_hbm, acount_s),
             (brow_hbm, brow_s), (bcol_hbm, bcol_s), (bcount_hbm, bcount_s))
    small = [pltpu.make_async_copy(source, target, local_sem.at[4 + i])
             for i, (source, target) in enumerate(pairs)]
    for copy in small + [own_b, own_a, own_keep]:
        copy.start()
    store[0] = jnp.zeros((BS, BS), jnp.bfloat16)
    acc[...] = jnp.zeros_like(acc)
    for copy in small:
        copy.wait()
    wide = lax.broadcasted_iota(jnp.int32, (1, IDS), 1)
    b_line = jnp.full((1, IDS), -1000, jnp.int32)
    for t in range(NZB):
        value = jnp.where(t < bcount_s[0, 0, 0], brow_s[t] * COLB + bcol_s[t], -1000)
        b_line = jnp.where(wide == row * PITCH + t, value, b_line)
    b_note[...] = b_line
    b_notes[row] = b_line
    a_rows_line = jnp.zeros((1, IDS), jnp.int32)
    a_line = jnp.full((1, LANES), -5000, jnp.int32)
    lane = lax.broadcasted_iota(jnp.int32, (1, LANES), 1)
    for s in range(NZA):
        live = s < acount_s[0, 0, 0]
        spot_at = jnp.where(live, col * KT + acol_s[s], -1)
        a_rows_line = jnp.where(wide == spot_at, 1, a_rows_line)
        value = jnp.where(live, acol_s[s] * COLB, -5000)
        a_line = jnp.where((lane >= s * COLB) & (lane < (s + 1) * COLB), value + lane - s * COLB, a_line)
        a_line = jnp.where(lane == NZA * COLB + s, arow_s[s], a_line)
    a_note[:, :IDS] = a_rows_line
    a_note[:, IDS:] = a_line
    a_notes[col] = a_note[...]
    pl.semaphore_wait(barrier, N_ROW - 1 + N_COL - 1 + N_DEPTH - 1)

    def toward(way):
        return {"row": row_peer(1 if way == RIGHT else N_ROW - 1)}

    def hop(way):
        return pltpu.make_async_remote_copy(
            src_ref=b_hbm, dst_ref=store.at[pl.ds(NEAR + way * NZB, NZB)],
            send_sem=hop_send.at[way], recv_sem=hop_recv.at[way],
            device_id=toward(way), device_id_type=MESH)

    def round_copy(way, k):
        return pltpu.make_async_remote_copy(
            src_ref=stage.at[way, k], dst_ref=landing.at[way, k],
            send_sem=round_send.at[way, k], recv_sem=round_recv.at[way, k],
            device_id=toward(way), device_id_type=MESH)

    def b_note_copy(k):
        return pltpu.make_async_remote_copy(
            src_ref=b_note, dst_ref=b_notes.at[row], send_sem=bn_send.at[k], recv_sem=bn_recv.at[k],
            device_id={"row": row_peer(k)}, device_id_type=MESH)

    def need_copy(k):
        return pltpu.make_async_remote_copy(
            src_ref=need_note, dst_ref=needs.at[row], send_sem=n_send.at[k], recv_sem=n_recv.at[k],
            device_id={"row": row_peer(k)}, device_id_type=MESH)

    def a_note_copy(k):
        return pltpu.make_async_remote_copy(
            src_ref=a_note, dst_ref=a_notes.at[col], send_sem=an_send.at[k], recv_sem=an_recv.at[k],
            device_id={"col": col_peer(k)}, device_id_type=MESH)

    def a_copy(k):
        return pltpu.make_async_remote_copy(
            src_ref=a_hbm, dst_ref=abuf.at[col], send_sem=a_send.at[k], recv_sem=a_recv.at[k],
            device_id={"col": col_peer(k)}, device_id_type=MESH)

    def flag_copy(k):
        return pltpu.make_async_remote_copy(
            src_ref=flag_note, dst_ref=flags.at[col], send_sem=f_send.at[k], recv_sem=f_recv.at[k],
            device_id={"col": col_peer(k)}, device_id_type=MESH)

    def depth_flag_copy(k):
        return pltpu.make_async_remote_copy(
            src_ref=depth_note, dst_ref=depth_flags.at[depth], send_sem=g_send.at[k], recv_sem=g_recv.at[k],
            device_id={"depth": depth_peer(k)}, device_id_type=MESH)

    for k in range(1, N_COL):
        a_note_copy(k).start()
    for k in FARTHEST:
        b_note_copy(k).start()

    for k in range(1, N_COL):
        a_note_copy(k).wait_recv()
    need = a_notes[0][:, :IDS]
    for c in range(1, N_COL):
        need = jnp.maximum(need, a_notes[c][:, :IDS])
    need_note[...] = need
    needs[row] = need
    for k in FARTHEST:
        need_copy(k).start()
    for way in (RIGHT, LEFT):
        hop(way).start()
    for k in range(1, N_COL):
        a_copy(k).start()

    for k in range(1, N_ROW):
        b_note_copy(k).wait_recv()
    blocks = b_notes[0]
    for r in range(1, N_ROW):
        blocks = jnp.maximum(blocks, b_notes[r])
    inner = jnp.where(blocks >= 0, (wide // PITCH) * KBT + blocks // COLB, -1)
    at_row = lax.broadcasted_iota(jnp.int32, (IDS, IDS), 0)
    spread = jnp.where(at_row == inner, 1.0, 0.0).astype(jnp.bfloat16)
    z = lax.broadcasted_iota(jnp.int32, (N_ROW, IDS), 0)
    ident = lax.broadcasted_iota(jnp.int32, (N_ROW, IDS), 1)
    origin, spot = ident // PITCH, ident % PITCH
    apart = ((z - origin + N_ROW) % N_ROW, (origin - z + N_ROW) % N_ROW)
    reach = (jnp.where(spot < HALF, FAR, FAR - 1), jnp.where(spot < HALF, FAR - 1, FAR))
    for k in range(1, N_ROW):
        need_copy(k).wait_recv()
    asked = jnp.concatenate([needs[r] for r in range(N_ROW)], axis=0)
    wanted = jnp.dot(asked.astype(jnp.float32).astype(jnp.bfloat16), spread, preferred_element_type=jnp.float32)
    left_to_go, where_at = [], []
    for way in (RIGHT, LEFT):
        inside = (wanted > 0.5) & (apart[way] >= 1) & (apart[way] <= reach[way])
        last = jnp.max(jnp.where(inside, apart[way], 0), axis=0, keepdims=True)
        left_to_go.append(jnp.where(apart[way] == 1, jnp.maximum(last - 1, 0), 0))
        where_at.append(jnp.where((apart[way] == 1) & (spot < NZB), NEAR + way * NZB + spot, 0))
    slot_of = lax.broadcasted_iota(jnp.int32, (N_ROW, LANES), 1)
    zero_plan = jnp.zeros((N_ROW, LANES), jnp.int32)

    waiting = [jnp.minimum(togo, 0) for togo in left_to_go for _ in range(LAG - 1)]

    def one_round(k, state):
        state = list(state)
        for way in (RIGHT, LEFT):
            togo, at, chosen = state[way], state[2 + way], state[4 + way]
            queue = state[6 + way * (LAG - 1):6 + (way + 1) * (LAG - 1)]
            moved = jnp.zeros_like(togo)
            landed = jnp.zeros_like(togo)
            for m in range(PER_ROUND):
                rank = jnp.where(togo > 0, togo * IDS + ident, 0)
                best = jnp.max(rank, axis=1, keepdims=True)
                pick = (rank == best) & (togo > 0)
                source = jnp.max(jnp.where(pick, at, 0), axis=1, keepdims=True)
                number = k * PER_ROUND + m
                chosen = jnp.where(slot_of == number, source, chosen)
                moved = jnp.where(pick, togo - 1, moved)
                landed = jnp.where(pick, FRESH + way * ROUNDS * PER_ROUND + number, landed)
                togo = jnp.where(pick, 0, togo)
            turn = 1 if way == RIGHT else N_ROW - 1
            queue = [pltpu.roll(moved, turn, 0), *queue]
            state[way] = togo + queue.pop()
            state[6 + way * (LAG - 1):6 + (way + 1) * (LAG - 1)] = queue
            state[2 + way] = jnp.maximum(at, pltpu.roll(landed, turn, 0))
            state[4 + way] = chosen
        return tuple(state)

    def plan_move(piece):
        return pltpu.make_async_copy(plan.at[piece], plan_s.at[piece], plan_sem.at[piece])

    def schedule(piece, first, last, state):
        state = lax.fori_loop(first, last, one_round, (*state[:4], zero_plan, zero_plan, *state[6:]))
        plan[piece, RIGHT] = state[4]
        plan[piece, LEFT] = state[5]
        plan_move(piece).start()
        return state

    state = schedule(0, 0, PIECES[0], (*left_to_go, *where_at, zero_plan, zero_plan, *waiting))
    own_b.wait()
    own_a.wait()
    own_keep.wait()
    for way in (RIGHT, LEFT):
        hop(way).wait_recv()

    def finish_schedule(state):
        own_at = jnp.where((apart[0] == 0) & (spot < NZB), OWN + spot, 0)
        final = jnp.maximum(jnp.maximum(state[2], state[3]), own_at)
        places[0] = final[:, :LANES]
        places[1] = final[:, LANES:]
        places_move.start()
        undone = jnp.maximum(state[0], state[1])
        for late in state[6:]:
            undone = jnp.maximum(undone, late)
        undone = jnp.max(undone, axis=0, keepdims=True)
        undone = jnp.maximum(undone[:, :LANES], undone[:, LANES:])
        flag_note[...] = undone
        flags[col] = undone
        for i in range(1, N_COL):
            flag_copy(i).start()

    def build_table():
        for c in range(N_COL):
            left = a_notes[c][:, IDS:]
            slot = jnp.full((1, LANES), PITCH - 1, jnp.int32)
            for h in range(2):
                for t in range(NZB):
                    at = (2 * c + h) * PITCH + t
                    slot = jnp.where(left == blocks[:, at:at + 1] + h * (KBT * COLB), at, slot)
            table[c] = jnp.where(lane < NZA * COLB, slot, left)
        move.start()

    def build_left(c):
        for s in range(NZA):
            block = abuf[c, s]
            which = table_s[c, 0, NZA * COLB + s]
            for i in range(ROWB):
                lhs[c, i * BS:(i + 1) * BS, s * BS:(s + 1) * BS] = jnp.where(
                    which == i, block, jnp.zeros_like(block))

    def share_flag():
        for i in range(1, N_COL):
            flag_copy(i).wait_recv()
        total = flags[0]
        for c in range(1, N_COL):
            total = jnp.maximum(total, flags[c])
        depth_note[...] = total
        depth_flags[depth] = total
        for i in range(1, N_DEPTH):
            depth_flag_copy(i).start()

    move = pltpu.make_async_copy(table, table_s, local_sem.at[2])
    places_move = pltpu.make_async_copy(places, places_s, local_sem.at[11])
    piece_of = [p for p, n in enumerate(PIECES) for _ in range(n)]
    starts = [sum(PIECES[:p]) for p in range(len(PIECES))]
    for k in range(ROUNDS + LAG):
        for way in (RIGHT, LEFT):
            if k >= LAG:
                round_copy(way, k - LAG).wait_recv()
                for m in range(PER_ROUND):
                    at = FRESH + (way * ROUNDS + k - LAG) * PER_ROUND + m
                    store[at] = landing[way, k - LAG, m]
            if k < ROUNDS and way == RIGHT and k in starts:
                plan_move(piece_of[k]).wait()
            if k < ROUNDS:
                for m in range(PER_ROUND):
                    stage[way, k, m] = store[plan_s[piece_of[k], way, row, k * PER_ROUND + m]]
                round_copy(way, k).start()
        if k + 1 < len(PIECES):
            state = schedule(k + 1, starts[k + 1], starts[k + 1] + PIECES[k + 1], state)
        if k + 1 == len(PIECES):
            finish_schedule(state)
        if k == len(PIECES):
            build_table()
        if k == len(PIECES) + 2:
            move.wait()
            for i in range(1, N_COL):
                a_copy(i).wait_recv()
        if len(PIECES) + 2 <= k < len(PIECES) + 2 + N_COL:
            build_left(k - len(PIECES) - 2)
        if k == len(PIECES) + 2 + N_COL:
            share_flag()
    places_move.wait()

    def part(j):
        for c in range(N_COL):
            strips = []
            for s in range(NZA):
                pair = []
                for e in range(2):
                    at = table_s[c, 0, s * COLB + 2 * j + e]
                    pair.append(store[places_s[at // LANES, row, at % LANES]])
                strips.append(jnp.concatenate(pair, axis=1))
            acc[j] += jnp.dot(lhs[c], jnp.concatenate(strips, axis=0), preferred_element_type=jnp.float32)


    def to_sibling(slot, half):
        part = pl.ds(half * BS, BS)
        which = across_sibling if slot == 0 else sibling
        return pltpu.make_async_remote_copy(
            src_ref=acc.at[which, part], dst_ref=rs1.at[slot, part],
            send_sem=d1_send.at[slot, half], recv_sem=d1_recv.at[slot, half],
            device_id={"depth": sibling}, device_id_type=MESH)

    def to_across(half):
        part = pl.ds(half * BS, BS)
        return pltpu.make_async_remote_copy(
            src_ref=acc.at[across, part], dst_ref=rs2.at[part],
            send_sem=d2_send.at[half], recv_sem=d2_recv.at[half],
            device_id={"depth": across}, device_id_type=MESH)

    part(across_sibling)
    for half in range(ROWB):
        to_sibling(0, half).start()
    part(across)
    for half in range(ROWB):
        span = pl.ds(half * BS, BS)
        to_sibling(0, half).wait_recv()
        acc[across, span] += rs1[0, span]
        to_across(half).start()
    part(sibling)
    for half in range(ROWB):
        to_sibling(1, half).start()
    part(depth)
    total = jnp.zeros((1, QUARTER), jnp.float32)
    for half in range(ROWB):
        span = pl.ds(half * BS, BS)
        to_sibling(1, half).wait_recv()
        mine = acc[depth, span] + rs1[1, span]
        to_across(half).wait_recv()
        product = mine + rs2[span]
        pruned = jnp.where(keep_ref[half:half + 1, :] > 0, product, 0.0)
        squares = pruned * pruned
        flow_ref[span] = squares
        total = total + jnp.sum(squares, axis=0, keepdims=True)
    colsum[...] = total
    masses[row] = total

    def mass_copy(k):
        return pltpu.make_async_remote_copy(
            src_ref=colsum, dst_ref=masses.at[row], send_sem=m_send.at[k], recv_sem=m_recv.at[k],
            device_id={"row": row_peer(k)}, device_id_type=MESH)

    for k in FARTHEST:
        mass_copy(k).start()
    for k in range(1, N_ROW):
        mass_copy(k).wait_recv()
    mass = jnp.sum(masses[...], axis=0) * (1.0 / (N_ROW * ROWS)) + epsilon
    flow_ref[...] = flow_ref[...] / mass

    for i in range(1, N_DEPTH):
        depth_flag_copy(i).wait_recv()
    over = depth_flags[0]
    for i in range(1, N_DEPTH):
        over = jnp.maximum(over, depth_flags[i])
    over_ref[0, 0] = jnp.max(over)

    for way in (RIGHT, LEFT):
        hop(way).wait_send()
        for k in range(ROUNDS):
            round_copy(way, k).wait_send()
    for k in range(1, N_ROW):
        b_note_copy(k).wait_send()
        need_copy(k).wait_send()
        mass_copy(k).wait_send()
    for k in range(1, N_COL):
        a_note_copy(k).wait_send()
        a_copy(k).wait_send()
        flag_copy(k).wait_send()
    for k in range(1, N_DEPTH):
        depth_flag_copy(k).wait_send()
    for half in range(ROWB):
        for slot in range(2):
            to_sibling(slot, half).wait_send()
        to_across(half).wait_send()


def shards(a_vals, a_rows, a_cols, a_count, b_vals, b_rows, b_cols, b_count, keep):
    vmem = pl.BlockSpec(memory_space=pltpu.VMEM)
    hbm = pl.BlockSpec(memory_space=pltpu.HBM)
    dma = pltpu.SemaphoreType.DMA
    inputs = (
        a_vals.reshape(NZA, BS, BS),
        a_rows.reshape(NZA),
        a_cols.reshape(NZA),
        a_count,
        b_vals.reshape(NZB, BS, BS),
        b_rows.reshape(NZB),
        b_cols.reshape(NZB),
        b_count,
        keep,
    )
    flow = jax.ShapeDtypeStruct((ROWS, QUARTER), jnp.float32)
    words = [
        pltpu.SMEM((NZA,), jnp.int32),
        pltpu.SMEM((NZA,), jnp.int32),
        pltpu.SMEM((1, 1, 1), jnp.int32),
        pltpu.SMEM((NZB,), jnp.int32),
        pltpu.SMEM((NZB,), jnp.int32),
        pltpu.SMEM((1, 1, 1), jnp.int32),
        pltpu.VMEM((ROWB, QUARTER), jnp.int32),
    ]
    sums = [
        pltpu.VMEM((N_DEPTH, ROWS, QUARTER), jnp.float32),
        pltpu.VMEM((2, ROWS, QUARTER), jnp.float32),
        pltpu.VMEM((ROWS, QUARTER), jnp.float32),
        pltpu.VMEM((1, QUARTER), jnp.float32),
        pltpu.VMEM((N_ROW, 1, QUARTER), jnp.float32),
    ]
    tail = [dma((2, ROWB))] * 2 + [dma((ROWB,))] * 2 + [dma((N_ROW,))] * 2
    left = [
        pltpu.VMEM((N_COL, NZA, BS, BS), jnp.bfloat16),
        pltpu.VMEM((N_COL, ROWS, NZA * BS), jnp.bfloat16),
    ]

    def full():
        return pl.pallas_call(
            full_ring,
            out_shape=flow,
            in_specs=[hbm] * 9,
            out_specs=vmem,
            scratch_shapes=[pltpu.VMEM((NZB + 1, BS, BS), jnp.bfloat16)] * N_ROW
            + words
            + [pltpu.VMEM((1, LANES), jnp.int32)] * 2
            + left
            + [
                pltpu.VMEM((N_COL, 1, LANES), jnp.int32),
                pltpu.VMEM((N_ROW, 1, LANES), jnp.int32),
                pltpu.VMEM((N_ROW, 1, LANES), jnp.int32),
                pltpu.SMEM((N_ROW, 1, LANES), jnp.int32),
            ]
            + sums
            + [dma((10,))]
            + [dma((2, FAR + 1, 2))] * 2
            + [dma((N_COL,))] * 4
            + [dma((N_ROW,))] * 2
            + tail,
            compiler_params=pltpu.CompilerParams(
                collective_id=1, has_side_effects=True, vmem_limit_bytes=64 << 20
            ),
        )(*inputs)

    result, over = pl.pallas_call(
        sparse_ring,
        out_shape=(flow, jax.ShapeDtypeStruct((1, 1), jnp.int32)),
        in_specs=[hbm] * 9,
        out_specs=(vmem, pl.BlockSpec(memory_space=pltpu.SMEM)),
        scratch_shapes=words
        + [
            pltpu.VMEM((1, IDS + LANES), jnp.int32),
            pltpu.VMEM((1, IDS), jnp.int32),
            pltpu.VMEM((1, IDS), jnp.int32),
        ]
        + left
        + [
            pltpu.VMEM((N_COL, 1, IDS + LANES), jnp.int32),
            pltpu.VMEM((N_ROW, 1, IDS), jnp.int32),
            pltpu.VMEM((N_ROW, 1, IDS), jnp.int32),
            pltpu.VMEM((N_COL, 1, LANES), jnp.int32),
            pltpu.SMEM((N_COL, 1, LANES), jnp.int32),
            pltpu.VMEM((len(PIECES), 2, N_ROW, LANES), jnp.int32),
            pltpu.SMEM((len(PIECES), 2, N_ROW, LANES), jnp.int32),
            pltpu.VMEM((2, N_ROW, LANES), jnp.int32),
            pltpu.SMEM((2, N_ROW, LANES), jnp.int32),
            pltpu.VMEM((HELD, BS, BS), jnp.bfloat16),
            pltpu.VMEM((2, ROUNDS, PER_ROUND, BS, BS), jnp.bfloat16),
            pltpu.VMEM((2, ROUNDS, PER_ROUND, BS, BS), jnp.bfloat16),
            pltpu.VMEM((1, LANES), jnp.int32),
            pltpu.VMEM((N_COL, 1, LANES), jnp.int32),
            pltpu.VMEM((1, LANES), jnp.int32),
            pltpu.VMEM((N_DEPTH, 1, LANES), jnp.int32),
        ]
        + sums
        + [dma((12,)), dma((len(PIECES),))]
        + [dma((2,))] * 2
        + [dma((2, ROUNDS))] * 2
        + [dma((N_COL,))] * 4
        + [dma((N_ROW,))] * 4
        + [dma((N_COL,))] * 2
        + [dma((N_DEPTH,))] * 2
        + tail,
        compiler_params=pltpu.CompilerParams(
            collective_id=0, has_side_effects=True, vmem_limit_bytes=64 << 20
        ),
    )(*inputs)
    return lax.cond(over[0, 0] > 0, full, lambda: result)


def solution(mesh):
    placed = (
        P("row", "depth", "col", None, None, None),
        P("row", "depth", "col", None),
        P("row", "depth", "col", None),
        P("row", "depth", "col"),
        P("depth", "row", "col", None, None, None),
        P("depth", "row", "col", None),
        P("depth", "row", "col", None),
        P("depth", "row", "col"),
        P("row", ("col", "depth")),
    )
    return jax.shard_map(
        shards, mesh=mesh, in_specs=placed, out_specs=P("row", ("col", "depth")), check_vma=False
    )
```
